32 devices in a mesh: gz: 4 (over y, x), gy: 8 (over z, core).
Axes of the slice: x: 2, y: 2, z: 4, core: 2. Of those that a mesh axis runs over, the one named last changes fastest.
Arguments:
- fixed: float32 [128, 512, 256], P('gz', 'gy'), may hold values from -6 to 6
- moving: float32 [128, 512, 256], P('gz', 'gy'), may hold values from -6 to 6
Outputs:
- update: float32 [3, 16, 64, 32], P(None, 'gz', 'gy')
- residual: float32 [3, 16, 64, 32], P(None, 'gz', 'gy')
The draws below stay inside these ranges and needn't reach their ends.
All inputs are finite; a program needn't handle non-finite values.
Results may differ from the reference program's by a relative error of at most 0.0031.
Values sent between devices are 32-bit elements; how exact they have to be, the bound alone decides.
No kernel may reach another device: no remote copies, remote signals or barrier semaphores. Data moves between devices by JAX's collectives and lax.ppermute only.
A program may use at most 64 MiB of HBM per device.

```python
import jax
import jax.numpy as jnp
from jax import lax

SPACING = 8
ITERS = 2
CZ = 32
CY = 64
NX = 256
NZ = 128
NY = 512
NCZ = 16
NCY = 64
NCX = 32
N_GZ = 4
N_GY = 8


def block_scale(stream_key, shape, shards, smallest, largest):
    level, own = 1.0, jax.random.fold_in(stream_key, 6)
    for axis_at, parts in shards:
        draws = jnp.exp(jax.random.uniform(jax.random.fold_in(own, axis_at), (parts,), jnp.float32, smallest / len(shards), largest / len(shards)))
        level = level * jnp.repeat(draws, shape[axis_at] // parts).reshape([-1 if axis == axis_at else 1 for axis in range(len(shape))])
    return level


def centred(rng, extent, deviation, reach, cuts=(), kind=jnp.bfloat16):
    result = deviation * jax.random.normal(rng, extent, jnp.float32)
    if cuts:
        result = result * block_scale(rng, extent, cuts, -0.22, 0.18)
    return jnp.clip(result, -reach, reach).astype(kind)


def setup_inputs(seed: int = 0) -> dict:
    key_list = jax.random.split(jax.random.key(seed), 3)
    fixed = centred(key_list[0], (NZ, NY, NX), 1.0, 6.0, ((0, 4), (1, 8)), jnp.float32)
    moving = centred(key_list[1], (NZ, NY, NX), 1.0, 6.0, ((0, 4), (1, 8)), jnp.float32)
    return {"fixed": fixed, "moving": moving}


damping_weight = 8.0


def basis_matrix(count, columns, offset):
    voxel = jnp.arange(count, dtype=jnp.int32)
    cell = voxel // SPACING
    frac = ((voxel % SPACING).astype(jnp.float32) + 0.5) / SPACING
    other = 1.0 - frac
    weights = (other ** 3 / 6.0, (3.0 * frac ** 3 - 6.0 * frac ** 2 + 4.0) / 6.0,
               (-3.0 * frac ** 3 + 3.0 * frac ** 2 + 3.0 * frac + 1.0) / 6.0, frac ** 3 / 6.0)
    index = jnp.arange(columns, dtype=jnp.int32)
    matrix = jnp.zeros((count, columns), jnp.float32)
    for tap in range(4):
        match = index[None, :] == (cell - 1 + tap + offset)[:, None]
        matrix = matrix + jnp.where(match, weights[tap][:, None], jnp.float32(0.0))
    return matrix


def decode(control, along_z, along_y, along_x):
    hp = lax.Precision.HIGHEST
    inner = jnp.einsum('cabe,xe->cabx', control, along_x, precision=hp)
    inner = jnp.einsum('yb,cabx->cayx', along_y, inner, precision=hp)
    return jnp.einsum('za,cayx->czyx', along_z, inner, precision=hp)


def encode(volume, along_z, along_y, along_x):
    hp = lax.Precision.HIGHEST
    inner = jnp.einsum('za,czyx->cayx', along_z, volume, precision=hp)
    inner = jnp.einsum('yb,cayx->cabx', along_y, inner, precision=hp)
    return jnp.einsum('xe,cabx->cabe', along_x, inner, precision=hp)


def derivative(padded, axis):
    length = padded.shape[axis] - 6

    def part(shift_by):
        return lax.slice_in_dim(padded, 3 + shift_by, 3 + shift_by + length, axis=axis)

    return (45.0 * (part(1) - part(-1)) - 9.0 * (part(2) - part(-2)) + (part(3) - part(-3))) / 60.0


def gradients(padded):
    return jnp.stack([derivative(padded[:, 3:-3, 3:-3], 0),
                      derivative(padded[3:-3, :, 3:-3], 1),
                      derivative(padded[3:-3, 3:-3, :], 2)])


def reference(fixed, moving):
    mean = 0.5 * (fixed + moving)
    gradient = gradients(jnp.pad(mean, 3)).astype(jnp.bfloat16)
    mismatch = moving - fixed
    ctrl_z = CZ // SPACING
    ctrl_y = CY // SPACING
    ctrl_x = NX // SPACING
    along_z = basis_matrix(CZ, ctrl_z + 4, 2)
    along_y = basis_matrix(CY, ctrl_y + 4, 2)
    along_x = basis_matrix(NX, ctrl_x, 0)
    zero = jnp.int32(0)

    def accumulate(control, with_data):
        padded = jnp.pad(control, ((0, 0), (2, 2), (2, 2), (0, 0)))

        def step(total, block):
            zb = block // N_GY
            yb = block % N_GY
            slab = lax.dynamic_slice(gradient, (zero, zb * CZ, yb * CY, zero), (3, CZ, CY, NX)).astype(jnp.float32)
            start = (zero, zb * ctrl_z, yb * ctrl_y, zero)
            shape = (3, ctrl_z + 4, ctrl_y + 4, ctrl_x)
            if with_data:
                local = lax.dynamic_slice(mismatch, (zb * CZ, yb * CY, zero), (CZ, CY, NX))
                volume = slab * local[None]
            else:
                field = decode(lax.dynamic_slice(padded, start, shape), along_z, along_y, along_x)
                volume = slab * jnp.sum(slab * field, axis=0)[None]
            back = encode(volume, along_z, along_y, along_x)
            current = lax.dynamic_slice(total, start, shape)
            return lax.dynamic_update_slice(total, current + back, start), None

        total, unused = lax.scan(step, jnp.zeros_like(padded), jnp.arange(N_GZ * N_GY, dtype=jnp.int32))
        return total[:, 2:-2, 2:-2, :]

    shape = (3, NCZ, NCY, NCX)
    rhs = -accumulate(jnp.zeros(shape, jnp.float32), True)
    update = jnp.zeros(shape, jnp.float32)
    residual = rhs
    direction = rhs
    norm_now = jnp.sum(residual * residual)
    for step_index in range(ITERS):
        image = accumulate(direction, False) + damping_weight * direction
        alpha = norm_now / jnp.sum(direction * image)
        update = update + alpha * direction
        residual = residual - alpha * image
        norm_next = jnp.sum(residual * residual)
        direction = residual + (norm_next / norm_now) * direction
        norm_now = norm_next
    return update, residual
```

```python
import functools

import jax
import jax.numpy as jnp
import numpy as np
from jax import lax
from jax.experimental import pallas as pl
from jax.experimental.pallas import tpu as pltpu
from jax.sharding import PartitionSpec as P

SPACING = 8
DAMPING = 8.0
LANES = 128
F32 = jnp.float32
BF16 = jnp.bfloat16
VMEM = pl.BlockSpec(memory_space=pltpu.VMEM)
PARAMS = pltpu.CompilerParams(vmem_limit_bytes=20 * 1024 * 1024)


def round_up(value, step):
    return -(-value // step) * step


class Sizes:
    def __init__(self, shape):
        self.sz, self.sy, self.nx = shape
        self.cz, self.cy, self.cx = (n // SPACING for n in shape)
        self.na, self.nb = self.cz + 3, self.cy + 3
        self.ap = round_up(self.na, 8)
        self.rows = self.nb * self.ap
        self.rp = round_up(self.rows, LANES)
        self.used = 3 * self.cx
        self.lp = round_up(self.used + 1, LANES)
        self.zface = round_up(3 * self.nb, 8)
        self.yface = 3 * self.ap
        self.own = self.cz * self.cy
        self.block = round_up(max(2 * self.cy, 2 * self.cz, 8), 8)


def taps():
    t = (np.arange(SPACING) + 0.5) / SPACING
    return np.stack(
        [
            (1 - t) ** 3 / 6,
            (3 * t**3 - 6 * t**2 + 4) / 6,
            (-3 * t**3 + 3 * t**2 + 3 * t + 1) / 6,
            t**3 / 6,
        ]
    )


def basis(count, columns, offset):
    w = taps()
    out = np.zeros((count, columns))
    for v in range(count):
        for k in range(4):
            col = v // SPACING - 1 + k + offset
            if 0 <= col < columns:
                out[v, col] += w[k, v % SPACING]
    return out


def halves(matrix):
    high = np.asarray(matrix, np.float32).astype(jnp.bfloat16)
    low = (matrix - high.astype(np.float64)).astype(np.float32).astype(jnp.bfloat16)
    return high, low


def decode_consts(s):
    by = basis(s.sy, s.nb, 1)
    kd = np.zeros((s.na * s.sy, s.rp))
    for a in range(s.na):
        for b in range(s.nb):
            kd[a * s.sy : (a + 1) * s.sy, b * s.ap + a] = by[:, b]
    kh, kl = halves(kd)
    xh, xl = halves(x_matrix(s))
    return (
        np.concatenate([kh, kh], 1),
        kl,
        np.concatenate([xh, xh], 0),
        xl,
    )


def x_matrix(s):
    bx = basis(s.nx, s.cx, 0)
    out = np.zeros((s.lp, 3 * s.nx))
    for c in range(3):
        out[c * s.cx : (c + 1) * s.cx, c * s.nx : (c + 1) * s.nx] = bx.T
    return out


def encode_x_consts(s):
    xh, xl = halves(x_matrix(s).T)
    return np.concatenate([xh, xl], 1), xh


def y_rows(s, order):
    by = basis(s.sy, s.nb, 1)
    out = np.zeros((len(order), s.na * s.sy))
    for row, item in enumerate(order):
        if item is not None:
            a, b = item
            out[row, a * s.sy : (a + 1) * s.sy] = by[:, b]
    return halves(out)


def padded(order, count):
    return order + [None] * (count - len(order))


def grid_order(s):
    return [(a, b) if a < s.na else None for b in range(s.nb) for a in range(s.ap)]


def exchange_order(s):
    down = [(k, b) for b in range(s.nb) for k in range(3)]
    up = [(s.cz + k, b) for b in range(s.nb) for k in range(3)]
    return grid_order(s) + padded(down, s.zface) + padded(up, s.zface)


def spans(count):
    return {
        -1: ([0], [count - 1]),
        0: (list(range(1, count + 1)), list(range(count))),
        1: ([count + 1, count + 2], [0, 1]),
    }


NEIGHBOURS = [(dz, dy) for dz in (-1, 0, 1) for dy in (-1, 0, 1) if dz or dy]


def message(s, dz, dy):
    za, ta = spans(s.cz)[dz]
    yb, tb = spans(s.cy)[dy]
    if dy == 0:
        return [(a, b) for a in za for b in yb], [(a, b) for a in ta for b in tb]
    return [(a, b) for b in yb for a in za], [(a, b) for b in tb for a in ta]


def final_order(s):
    order = [(a + 1, b + 1) for a in range(s.cz) for b in range(s.cy)]
    starts = []
    for dz, dy in NEIGHBOURS:
        starts.append(len(order))
        mine = message(s, dz, dy)[0]
        order = order + padded(mine, round_up(len(mine), 8))
    return order, starts


def gradient_consts(s):
    coef = {-3: -1.0, -2: 9.0, -1: -45.0, 1: 45.0, 2: -9.0, 3: 1.0}
    dx = np.zeros((s.nx, s.nx))
    for x in range(s.nx):
        for d, value in coef.items():
            if 0 <= x + d < s.nx:
                dx[x + d, x] = value
    dy = np.zeros((s.sy, s.sy + 16))
    for y in range(s.sy):
        for d, value in coef.items():
            at = y + d
            if at < 0:
                dy[y, s.sy + 3 + at] = value
            elif at >= s.sy:
                dy[y, s.sy + 3 + at - s.sy] = value
            else:
                dy[y, at] = value
    return dx.astype(jnp.bfloat16), dy.astype(jnp.bfloat16)


def split(value):
    high = value.astype(BF16)
    return high, (value - high.astype(F32)).astype(BF16)


def dot(a, b):
    return jnp.dot(a, b, preferred_element_type=F32)


def place(axis):
    index = lax.axis_index(axis)
    count = lax.axis_size(axis)
    return index, index > 0, index < count - 1, lax.rem(index, 2) == 0


def z_weights():
    w = taps()
    even = 0.5 * (w[0] + w[3])
    odd0 = 0.5 * (w[0] - w[3])
    odd1 = 0.5 * (w[1] - w[2])
    return [(float(even[k]), float(odd0[k]), float(odd1[k])) for k in range(SPACING // 2)]


def encode_cell(volume):
    sums = None
    for k, (ev, o0, o1) in enumerate(z_weights()):
        near, far = volume(k)
        new = []
        for c in range(3):
            e = near[c] + far[c]
            o = near[c] - far[c]
            new.append((e, ev * e, o0 * o, o1 * o))
        if sums is None:
            sums = new
        else:
            sums = [tuple(x + y for x, y in zip(old, add)) for old, add in zip(sums, new)]
    out = []
    for total, outer, o0, o1 in sums:
        inner = 0.5 * total - outer
        out.append((outer + o0, inner + o1, inner - o1, outer - o0))
    return out


def decode_cell(p):
    parts = []
    for p0, p1, p2, p3 in p:
        s12 = p1 + p2
        parts.append((0.5 * s12, (p0 + p3) - s12, p0 - p3, p1 - p2))
    weights = z_weights()

    def at(k):
        ev, o0, o1 = weights[k]
        near, far = [], []
        for half, outer, d03, d12 in parts:
            even = half + ev * outer
            odd = o0 * d03 + o1 * d12
            near.append(even + odd)
            far.append(even - odd)
        return near, far

    return at


def decode_xy(control, consts, f_ref):
    yh_ref, yl_ref, xh_ref, xl_ref = consts
    ph, plow = split(control)
    inner = dot(yh_ref[...], jnp.concatenate([ph, plow], 0)) + dot(yl_ref[...], ph)
    ih, il = split(inner)
    f_ref[...] = dot(jnp.concatenate([ih, il], 1), xh_ref[...]) + dot(ih, xl_ref[...])


def encode_xy(e_ref, x_consts, y_consts):
    xw_ref, xh_ref = x_consts
    yh_ref, yl_ref = y_consts
    eh, el = split(e_ref[...])
    wide = dot(eh, xw_ref[...])
    lp = wide.shape[1] // 2
    inner = wide[:, :lp] + wide[:, lp:] + dot(el, xh_ref[...])
    ih, il = split(inner)
    wide = dot(yh_ref[...], jnp.concatenate([ih, il], 1))
    return wide[:, :lp] + wide[:, lp:] + dot(yl_ref[...], ih)


def store_rows(e_ref, s, a, y0, lane, values):
    for c in range(3):
        e_ref[pl.ds(a * s.sy + y0, 8), pl.ds(c * s.nx + lane, LANES)] = values[c]


def load_rows(f_ref, s, a, y0, lane):
    return [
        f_ref[pl.ds(a * s.sy + y0, 8), pl.ds(c * s.nx + lane, LANES)] for c in range(3)
    ]


def gradient_planes(s, planes, near, s_plane, halo_ref, dx_ref, dy_ref, put):
    dx = dx_ref[...]
    dy = dy_ref[...]
    scale = F32(1.0 / 120.0)

    def step(i, carry):
        centre = near(i, 0)
        sh, sl = split(centre)
        hh, hl = split(halo_ref[s_plane(i)])
        gx = dot(sh, dx) + dot(sl, dx)
        gy = dot(dy, jnp.concatenate([sh, hh], 0)) + dot(dy, jnp.concatenate([sl, hl], 0))
        gz = (
            45.0 * (near(i, 1) - near(i, -1))
            - 9.0 * (near(i, 2) - near(i, -2))
            + (near(i, 3) - near(i, -3))
        )
        for c, value in enumerate((gz, gy, gx)):
            put(i, c, (value * scale).astype(BF16).astype(F32))
        return carry

    lax.fori_loop(0, planes, step, 0)


def mid_kernel(s, f_ref, m_ref, sum_ref, ra_ref, rb_ref, dx_ref, dy_ref, g_ref, e_ref, h_ref):
    _, below, above, even = place("gy")
    h_ref[...] = jnp.zeros_like(h_ref)
    for k in range(3):
        a, b = ra_ref[k], rb_ref[k]
        up = jnp.where(even, a, b)
        down = jnp.where(even, b, a)
        h_ref[:, k, :] = jnp.where(below, down, 0.0)
        h_ref[:, 3 + k, :] = jnp.where(above, up, 0.0)
    first = SPACING

    def put(i, c, value):
        g_ref[c, i] = value

    gradient_planes(
        s,
        s.sz - 2 * SPACING,
        lambda i, d: sum_ref[first + i + d],
        lambda i: first + i,
        h_ref,
        dx_ref,
        dy_ref,
        put,
    )

    def tile(t, carry):
        y0 = pl.multiple_of(t * 8, 8)
        for lane in range(0, s.nx, LANES):
            rows, cols = pl.ds(y0, 8), pl.ds(lane, LANES)
            pend = None
            for zc in range(1, s.cz - 1):

                def volume(k):
                    out = []
                    for v in (k, SPACING - 1 - k):
                        z = zc * SPACING + v
                        mm = f_ref[z, rows, cols] - m_ref[z, rows, cols]
                        out.append([mm * g_ref[c, z - first, rows, cols] for c in range(3)])
                    return out

                new = encode_cell(volume)
                if pend is not None:
                    new = [
                        (p[0] + n[0], p[1] + n[1], p[2] + n[2], n[3]) for p, n in zip(pend, new)
                    ]
                store_rows(e_ref, s, zc - 1, y0, lane, [n[0] for n in new])
                pend = [n[1:] for n in new]
            for k in range(3):
                store_rows(e_ref, s, s.cz - 2 + k, y0, lane, [p[k] for p in pend])
        return carry

    lax.fori_loop(0, s.sy // 8, tile, 0)


def edge_kernel(
    s, f_ref, m_ref, sum_ref, ra_ref, rb_ref, h_ref, em_ref, dx_ref, dy_ref,
    xw_ref, xh_ref, yh_ref, yl_ref, g_ref, p_ref, za_ref, zb_ref, t_ref, e_ref,
):
    _, below, above, even = place("gz")
    span = SPACING + 6
    for k in range(3):
        a, b = ra_ref[k], rb_ref[k]
        t_ref[k] = jnp.where(below, jnp.where(even, b, a), 0.0)
        t_ref[2 * span - 3 + k] = jnp.where(above, jnp.where(even, a, b), 0.0)
    t_ref[3:span] = sum_ref[0 : span - 3]
    t_ref[span : 2 * span - 3] = sum_ref[s.sz - span + 3 : s.sz]

    for side in range(2):
        base = side * span + 3
        shift = side * SPACING
        plane = 0 if side == 0 else s.sz - SPACING

        def put(i, c, value, shift=shift):
            g_ref[c, i + shift] = value

        gradient_planes(
            s,
            SPACING,
            lambda i, d, base=base: t_ref[base + i + d],
            lambda i, plane=plane: plane + i,
            h_ref,
            dx_ref,
            dy_ref,
            put,
        )

    def tile(t, carry):
        y0 = pl.multiple_of(t * 8, 8)
        for lane in range(0, s.nx, LANES):
            rows, cols = pl.ds(y0, 8), pl.ds(lane, LANES)
            layers = [None] * s.na
            for a in range(1, s.cz + 2):
                layers[a] = load_rows(em_ref, s, a - 1, y0, lane)
            for side, zc in ((0, 0), (1, s.cz - 1)):

                def volume(k):
                    out = []
                    for v in (k, SPACING - 1 - k):
                        z = zc * SPACING + v
                        mm = f_ref[z, rows, cols] - m_ref[z, rows, cols]
                        out.append(
                            [mm * g_ref[c, side * SPACING + v, rows, cols] for c in range(3)]
                        )
                    return out

                new = encode_cell(volume)
                for k in range(4):
                    a = zc + k
                    add = [n[k] for n in new]
                    old = layers[a]
                    layers[a] = add if old is None else [x + y for x, y in zip(old, add)]
            for a in range(s.na):
                store_rows(e_ref, s, a, y0, lane, layers[a])
        return carry

    lax.fori_loop(0, s.sy // 8, tile, 0)
    send_faces(s, encode_xy(e_ref, (xw_ref, xh_ref), (yh_ref, yl_ref)), p_ref, za_ref, zb_ref)


def send_faces(s, rows, p_ref, za_ref, zb_ref):
    even = place("gz")[3]
    p_ref[...] = rows[: s.rows]
    down = rows[s.rows : s.rows + s.zface]
    up = rows[s.rows + s.zface :]
    za_ref[...] = jnp.where(even, up, down)
    zb_ref[...] = jnp.where(even, down, up)


def fold_z_kernel(s, p_ref, ra_ref, rb_ref, o_ref, ya_ref, yb_ref, t_ref):
    _, below, above, even = place("gz")
    layer = lax.broadcasted_iota(jnp.int32, (s.rows, s.lp), 0) % s.ap
    first = jnp.where(below, 0, 1)
    last = jnp.where(above, s.cz + 2, s.cz)
    inside = (layer >= first) & (layer <= last)
    t_ref[...] = jnp.where(inside, p_ref[...], 0.0)
    a, b = ra_ref[...], rb_ref[...]
    up = jnp.where(above, jnp.where(even, a, b), 0.0)
    down = jnp.where(below, jnp.where(even, b, a), 0.0)
    for k in range(s.nb):
        low = k * s.ap
        t_ref[low : low + 3, :] += down[3 * k : 3 * k + 3, :]
        t_ref[low + s.cz : low + s.cz + 3, :] += up[3 * k : 3 * k + 3, :]
    total = t_ref[...]
    o_ref[...] = total
    even = place("gy")[3]
    down, up = total[: s.yface], total[s.cy * s.ap : s.cy * s.ap + s.yface]
    ya_ref[...] = jnp.where(even, up, down)
    yb_ref[...] = jnp.where(even, down, up)


def fold_y(s, p_ref, ra_ref, rb_ref, v_ref):
    _, below, above, even = place("gy")
    v_ref[...] = jnp.zeros_like(v_ref)
    v_ref[: s.rows, :] = p_ref[...]
    a, b = ra_ref[...], rb_ref[...]
    up, down = jnp.where(even, a, b), jnp.where(even, b, a)
    v_ref[: s.yface, :] += down
    high = s.cy * s.ap
    v_ref[high : high + s.yface, :] += up

    @pl.when(jnp.logical_not(below))
    def _():
        v_ref[: s.yface, :] = p_ref[: s.yface, :]
        v_ref[: s.ap, :] = jnp.zeros((s.ap, s.lp), F32)

    @pl.when(jnp.logical_not(above))
    def _():
        v_ref[high : high + s.yface, :] = p_ref[high : high + s.yface, :]
        v_ref[high + s.ap : high + s.yface, :] = jnp.zeros((s.yface - s.ap, s.lp), F32)


def own_part(s, v_ref, out_ref):
    for a in range(s.cz):
        out_ref[a * s.cy : (a + 1) * s.cy, :] = v_ref[pl.ds(s.ap + a + 1, s.cy, stride=s.ap), :]


def operate(s, v_ref, decode, g_mid, g_edge, f_ref, e_ref):
    decode_xy(v_ref[...], decode, f_ref)

    def tile(t, square):
        y0 = pl.multiple_of(t * 8, 8)
        for lane in range(0, s.nx, LANES):
            rows, cols = pl.ds(y0, 8), pl.ds(lane, LANES)
            pend = None
            layers = [load_rows(f_ref, s, a, y0, lane) for a in range(3)]
            for zc in range(s.cz):
                layers = layers[-3:] + [load_rows(f_ref, s, zc + 3, y0, lane)]
                field = decode_cell([[layers[i][c] for i in range(4)] for c in range(3)])
                if zc == 0:
                    g_ref, base = g_edge, 0
                elif zc == s.cz - 1:
                    g_ref, base = g_edge, SPACING
                else:
                    g_ref, base = g_mid, (zc - 1) * SPACING
                squares = []

                def volume(k):
                    out = []
                    for v, value in zip((k, SPACING - 1 - k), field(k)):
                        g = [g_ref[c, base + v, rows, cols] for c in range(3)]
                        dotted = g[0] * value[0] + g[1] * value[1] + g[2] * value[2]
                        squares.append(dotted * dotted)
                        out.append([g[c] * dotted for c in range(3)])
                    return out

                new = encode_cell(volume)
                for value in squares:
                    square = square + value
                if pend is not None:
                    new = [
                        (p[0] + n[0], p[1] + n[1], p[2] + n[2], n[3]) for p, n in zip(pend, new)
                    ]
                store_rows(e_ref, s, zc, y0, lane, [n[0] for n in new])
                pend = [n[1:] for n in new]
            for k in range(3):
                store_rows(e_ref, s, s.cz + k, y0, lane, [p[k] for p in pend])
        return square

    return lax.fori_loop(0, s.sy // 8, tile, jnp.zeros((8, LANES), F32))


def total_of(value):
    return jnp.sum(value, keepdims=True)


def apply_kernel(
    s, p_ref, ra_ref, rb_ref, gm_ref, ge_ref, d0, d1, d2, d3,
    xw_ref, xh_ref, yh_ref, yl_ref,
    o_ref, za_ref, zb_ref, own_ref, sum_ref, v_ref, f_ref, e_ref,
):
    fold_y(s, p_ref, ra_ref, rb_ref, v_ref)
    own_part(s, v_ref, own_ref)
    square = operate(s, v_ref, (d0, d1, d2, d3), gm_ref, ge_ref, f_ref, e_ref)
    send_faces(s, encode_xy(e_ref, (xw_ref, xh_ref), (yh_ref, yl_ref)), o_ref, za_ref, zb_ref)
    own = own_ref[...]
    sums = [total_of(own * own), total_of(square)]
    sum_ref[...] = moments(sums, 0)


def moments(sums, start):
    row = lax.broadcasted_iota(jnp.int32, (8, LANES), 0)
    out = jnp.zeros((8, LANES), F32)
    for k, value in enumerate(sums):
        out = jnp.where(row == start + k, value, out)
    return out


def last_kernel(
    s, starts, p_ref, ra_ref, rb_ref, gm_ref, ge_ref, m_ref, d0, d1, d2, d3,
    xw_ref, xh_ref, yh_ref, yl_ref,
    own_ref, part_ref, send_ref, v_ref, f_ref, e_ref,
):
    fold_y(s, p_ref, ra_ref, rb_ref, v_ref)
    own_part(s, v_ref, own_ref)
    square = operate(s, v_ref, (d0, d1, d2, d3), gm_ref, ge_ref, f_ref, e_ref)
    rows = encode_xy(e_ref, (xw_ref, xh_ref), (yh_ref, yl_ref))
    part_ref[...] = rows[: s.own]
    own = own_ref[...]
    sums = m_ref[...] + moments([total_of(own * own), total_of(square)], 2)
    free = lax.broadcasted_iota(jnp.int32, (8, s.lp), 1) >= s.used
    for d in range(send_ref.shape[0]):
        send_ref[d, 0:8, :] = sums
    iz, iy = lax.axis_index("gz"), lax.axis_index("gy")
    nz, ny = lax.axis_size("gz"), lax.axis_size("gy")
    for (dz, dy), start in zip(NEIGHBOURS, starts):
        count = round_up(len(message(s, dz, dy)[0]), 8)
        tz, ty = iz + dz, iy + dy
        ok = (tz >= 0) & (tz < nz) & (ty >= 0) & (ty < ny)

        @pl.when(ok)
        def _(start=start, count=count, target=tz * ny + ty):
            send_ref[target, 0:8, :] = jnp.where(free, sums, rows[start : start + 8])
            if count > 8:
                send_ref[target, 8:count, :] = rows[start + 8 : start + count]


def finish_kernel(s, v0_ref, v1_ref, part_ref, got_ref, u_ref, r_ref, t_ref):
    iz, iy = lax.axis_index("gz"), lax.axis_index("gy")
    nz, ny = lax.axis_size("gz"), lax.axis_size("gy")
    t_ref[...] = part_ref[...]
    for dz, dy in NEIGHBOURS:
        target = message(s, -dz, -dy)[1]
        tz, ty = iz + dz, iy + dy
        ok = (tz >= 0) & (tz < nz) & (ty >= 0) & (ty < ny)

        @pl.when(ok)
        def _(target=target, source=tz * ny + ty):
            row = 0
            while row < len(target):
                a, b = target[row]
                run = 1
                while row + run < len(target) and target[row + run] == (a, b + run):
                    run += 1
                at = a * s.cy + b
                t_ref[at : at + run, :] += got_ref[source, row : row + run, :]
                row += run

    tot = got_ref[0, 0:8, :]
    for d in range(1, got_ref.shape[0]):
        tot = tot + got_ref[d, 0:8, :]
    m0, m1, m2, m3 = (tot[k : k + 1, s.used : s.used + 1] for k in range(4))
    v0, v1, v2 = v0_ref[...], v1_ref[...], t_ref[...]
    rho = m1 / m0
    a0 = 1.0 / (rho + DAMPING)
    rr1 = a0 * a0 * (m2 - rho * m1)
    beta = rr1 / m0
    quad = a0 * a0 * (m3 - 2.0 * rho * m2 + rho * rho * m1) + DAMPING * rr1
    a1 = rr1 / (quad - beta * rr1 / a0)
    r1 = a0 * (rho * v0 - v1)
    image = a0 * (rho * v1 - v2) + DAMPING * r1 + beta * (v1 + DAMPING * v0)
    update = a0 * v0 + a1 * (r1 + beta * v0)
    residual = r1 - a1 * image
    for c in range(3):
        lanes = slice(c * s.cx, (c + 1) * s.cx)
        for a in range(s.cz):
            at = slice(a * s.cy, (a + 1) * s.cy)
            u_ref[c, a] = update[at, lanes]
            r_ref[c, a] = residual[at, lanes]


def swap(value_a, value_b, axis):
    count = lax.axis_size(axis)
    even = [(i, i ^ 1) for i in range(count)]
    odd = [(i, (i + (1 if i % 2 else -1)) % count) for i in range(count)]
    return lax.ppermute(value_a, axis, even), lax.ppermute(value_b, axis, odd)


def faces(fixed, moving, axis, dim):
    even = lax.rem(lax.axis_index(axis), 2) == 0
    high = fixed.shape[dim] - 3
    out = []
    for start in (jnp.where(even, high, 0), jnp.where(even, 0, high)):
        pair = [lax.dynamic_slice_in_dim(v, start, 3, dim) for v in (fixed, moving)]
        out.append(jnp.moveaxis(pair[0] + pair[1], dim, 0))
    return out


def call(kernel, name, outs, scratch, *args):
    shapes = [jax.ShapeDtypeStruct(o, F32) for o in outs]
    return pl.pallas_call(
        kernel,
        out_shape=shapes,
        in_specs=[VMEM] * len(args),
        out_specs=[VMEM] * len(outs),
        scratch_shapes=[pltpu.VMEM(n, F32) for n in scratch],
        compiler_params=PARAMS,
        name=name,
    )(*args)


def shards(fixed, moving):
    s = Sizes(fixed.shape)
    devices = lax.axis_size("gz") * lax.axis_size("gy")
    dx, dy = (jnp.asarray(v) for v in gradient_consts(s))
    decode = tuple(jnp.asarray(v) for v in decode_consts(s))
    encode_x = tuple(jnp.asarray(v) for v in encode_x_consts(s))
    encode_y = tuple(jnp.asarray(v) for v in y_rows(s, exchange_order(s)))
    order, starts = final_order(s)
    encode_last = tuple(jnp.asarray(v) for v in y_rows(s, order))

    ya, yb = swap(*faces(fixed, moving, "gy", 1), "gy")
    za, zb = swap(*faces(fixed, moving, "gz", 0), "gz")
    total = fixed + moving
    mid = s.sz - 2 * SPACING
    wide = (s.na * s.sy, 3 * s.nx)
    g_mid, e_mid, halo = call(
        functools.partial(mid_kernel, s),
        "mid",
        [(3, mid, s.sy, s.nx), ((s.cz + 1) * s.sy, 3 * s.nx), (s.sz, 16, s.nx)],
        [],
        fixed, moving, total, ya, yb, dx, dy,
    )
    grid = (s.rows, s.lp)
    zshape, yshape = (s.zface, s.lp), (s.yface, s.lp)
    g_edge, part, za, zb = call(
        functools.partial(edge_kernel, s),
        "edge",
        [(3, 2 * SPACING, s.sy, s.nx), grid, zshape, zshape],
        [(2 * (SPACING + 6), s.sy, s.nx), wide],
        fixed, moving, total, za, zb, halo, e_mid, dx, dy, *encode_x, *encode_y,
    )

    def fold_z(part, za, zb):
        za, zb = swap(za, zb, "gz")
        return call(
            functools.partial(fold_z_kernel, s), "fold_z", [grid, yshape, yshape], [grid], part, za, zb
        )

    part, ya, yb = fold_z(part, za, zb)
    ya, yb = swap(ya, yb, "gy")
    own = (s.own, s.lp)
    part, za, zb, v0, sums = call(
        functools.partial(apply_kernel, s),
        "apply",
        [grid, zshape, zshape, own, (8, LANES)],
        [(s.rp, s.lp), wide, wide],
        part, ya, yb, g_mid, g_edge, *decode, *encode_x, *encode_y,
    )
    part, ya, yb = fold_z(part, za, zb)
    ya, yb = swap(ya, yb, "gy")
    v1, part, send = call(
        functools.partial(last_kernel, s, starts),
        "last",
        [own, own, (devices, s.block, s.lp)],
        [(s.rp, s.lp), wide, wide],
        part, ya, yb, g_mid, g_edge, sums, *decode, *encode_x, *encode_last,
    )
    got = lax.all_to_all(send, ("gz", "gy"), 0, 0)
    out = (3, s.cz, s.cy, s.cx)
    return tuple(
        call(functools.partial(finish_kernel, s), "finish", [out, out], [own], v0, v1, part, got)
    )


def solution(mesh):
    return jax.shard_map(
        shards,
        mesh=mesh,
        in_specs=(P("gz", "gy", None), P("gz", "gy", None)),
        out_specs=(P(None, "gz", "gy", None), P(None, "gz", "gy", None)),
        check_vma=False,
    )
```

```python
import functools

import jax
import jax.numpy as jnp
import numpy as np
from jax import lax
from jax.experimental import pallas as pl
from jax.experimental.pallas import tpu as pltpu
from jax.sharding import PartitionSpec as P

SPACING = 8
DAMPING = 8.0
LANES = 128
REACH = 3
F32 = jnp.float32
BF16 = jnp.bfloat16
VMEM = pl.BlockSpec(memory_space=pltpu.VMEM)
HBM = pl.BlockSpec(memory_space=pltpu.MemorySpace.HBM)
PARAMS = pltpu.CompilerParams(vmem_limit_bytes=20 * 1024 * 1024)


def round_up(value, step):
    return -(-value // step) * step


class Sizes:
    def __init__(self, shape):
        self.sz, self.sy, self.nx = shape
        self.cz, self.cy, self.cx = (n // SPACING for n in shape)
        self.na, self.nb = self.cz + 3, self.cy + 3
        self.bp = round_up(self.nb, 16)
        self.per = round_up(self.na * self.cx, LANES)
        self.wide = 3 * self.per
        self.tap = 4 * self.cx
        self.face = round_up(REACH * self.cx, LANES)
        self.used = REACH * self.cx
        self.own = self.cz * self.cx
        self.cells = 3 * self.cz * self.sy
        self.pair = 2 * self.cx
        self.block = round_up(3 * self.pair + 1, LANES)
        assert self.tap % LANES == 0 and self.own % LANES == 0
        assert self.cy % 8 == 0 and self.bp == self.cy + 8 and self.cz > 1


def taps():
    t = (np.arange(SPACING) + 0.5) / SPACING
    return np.stack(
        [
            (1 - t) ** 3 / 6,
            (3 * t**3 - 6 * t**2 + 4) / 6,
            (-3 * t**3 + 3 * t**2 + 3 * t + 1) / 6,
            t**3 / 6,
        ]
    )


def basis(count, columns, offset):
    w = taps()
    out = np.zeros((count, columns))
    for v in range(count):
        for k in range(4):
            col = v // SPACING - 1 + k + offset
            if 0 <= col < columns:
                out[v, col] += w[k, v % SPACING]
    return out


def halves(matrix):
    high = np.asarray(matrix, np.float32).astype(jnp.bfloat16)
    low = (matrix - high.astype(np.float64)).astype(np.float32).astype(jnp.bfloat16)
    return high, low


def consts(s):
    by = basis(s.sy, s.bp, 1)
    yh, yl = halves(by)
    y_decode = np.concatenate([yh, yh, yl], 1)
    y_encode = np.concatenate([yh.T, yh.T, yl.T], 1)
    bx = basis(s.nx, s.cx, 0)
    w = taps()
    decode, encode = [], []
    for k in range(SPACING):
        high, low = halves(np.concatenate([w[t, k] * bx.T for t in range(4)], 0))
        encode.append(np.concatenate([high.T, low.T], 1))
    for sign in (1.0, -1.0):
        for k in range(SPACING // 2):
            parts = [0.5 * (w[t, k] + sign * w[3 - t, k]) * bx.T for t in range(2)]
            (h0, l0), (h1, l1) = (halves(v) for v in parts)
            flip = np.asarray(sign, jnp.bfloat16)
            zero = np.zeros((2 * s.cx, s.nx), jnp.bfloat16)
            decode.append(np.concatenate([h0, h1, flip * l1, flip * l0, h0, h1, zero], 0))
    return tuple(jnp.asarray(v) for v in (y_decode, np.stack(decode), y_encode, np.stack(encode)))


def gradient_consts(s):
    coef = {-3: -1.0, -2: 9.0, -1: -45.0, 1: 45.0, 2: -9.0, 3: 1.0}
    dx = np.zeros((s.nx, s.nx))
    for x in range(s.nx):
        for d, value in coef.items():
            if 0 <= x + d < s.nx:
                dx[x + d, x] = value
    dy = np.zeros((s.sy, s.sy + 16))
    for y in range(s.sy):
        for d, value in coef.items():
            at = y + d
            if at < 0:
                dy[y, s.sy + REACH + at] = value
            elif at >= s.sy:
                dy[y, s.sy + REACH + at - s.sy] = value
            else:
                dy[y, at] = value
    dx, dy = (v.astype(jnp.bfloat16) for v in (dx, dy))
    return jnp.asarray(np.concatenate([dx, dx], 0)), jnp.asarray(np.concatenate([dy, dy], 1))


def split(value):
    high = value.astype(BF16)
    return high, (value - high.astype(F32)).astype(BF16)


def dot(a, b):
    return jnp.dot(a, b, preferred_element_type=F32)


def rounded(value):
    return (value * F32(1.0 / 120.0)).astype(BF16).astype(F32)


def place(axis):
    index = lax.axis_index(axis)
    count = lax.axis_size(axis)
    return index > 0, index < count - 1, lax.rem(index, 2) == 0


def from_sides(even, a, b):
    return jnp.where(even, a, b), jnp.where(even, b, a)


def difference(near):
    return (
        45.0 * (near(1) - near(-1)) - 9.0 * (near(2) - near(-2)) + (near(3) - near(-3))
    )


def iota(shape, dim):
    return lax.broadcasted_iota(jnp.int32, shape, dim)


def roll(value, shift):
    shift = shift % value.shape[1]
    return pltpu.roll(value, shift, 1) if shift else value


def start_all(copies):
    for copy in copies:
        copy.start()
    return copies


def faces_z_kernel(s, f_ref, m_ref, za_ref, zb_ref, t_ref, sems):
    copies = []
    for i, ref in enumerate((f_ref, m_ref)):
        for j in range(2):
            z = pl.ds(j * (s.sz - REACH), REACH)
            copies.append(pltpu.make_async_copy(ref.at[z], t_ref.at[i, j], sems.at[i, j]))
    for copy in start_all(copies):
        copy.wait()
    even = place("gz")[2]
    down, up = (t_ref[0, j] + t_ref[1, j] for j in range(2))
    za_ref[...] = jnp.where(even, up, down)
    zb_ref[...] = jnp.where(even, down, up)


def faces_y_kernel(s, f_ref, m_ref, ya_ref, yb_ref):
    even = place("gy")[2]
    for k in range(REACH):
        high = s.sy - REACH + k
        down = f_ref[:, k, :] + m_ref[:, k, :]
        up = f_ref[:, high, :] + m_ref[:, high, :]
        ya_ref[k] = jnp.where(even, up, down)
        yb_ref[k] = jnp.where(even, down, up)


GROUP = 4


def start_kernel(s, f_ref, m_ref, dx_ref, sum_ref, diff_ref, gx_ref, gz_ref):
    dx = dx_ref[...]
    for i in range(s.sz // GROUP):
        planes = slice(i * GROUP, (i + 1) * GROUP)
        f, m = f_ref[planes], m_ref[planes]
        total = f + m
        sum_ref[planes] = total
        diff_ref[planes] = f - m
        sh, sl = split(total.reshape(GROUP * s.sy, s.nx))
        gx = rounded(dot(jnp.concatenate([sh, sl], 1), dx))
        gx_ref[planes] = gx.reshape(GROUP, s.sy, s.nx)

    def step(i, carry):
        for y in range(0, s.sy, 16):
            rows = slice(y, y + 16)
            gz_ref[i, rows] = rounded(difference(lambda d: sum_ref[i + REACH + d, rows]))
        return carry

    lax.fori_loop(0, s.sz - 2 * REACH, step, 0)


def edge_planes(s):
    return [z < REACH or z >= s.sz - REACH for z in range(s.sz)]


def put_volume(s, row, z, rows, diff_ref, grads, high_ref, low_ref):
    mm = diff_ref[z, rows]
    for c in range(3):
        high, low = split(mm * grads[c])
        at = slice(row + c * s.sy + rows.start, row + c * s.sy + rows.stop)
        high_ref[at, :] = high
        low_ref[at, :] = low


def inner_kernel(
    s, sum_ref, diff_ref, gx_ref, gz_ref, ra_ref, rb_ref, dy_ref, re_ref,
    gy_ref, acc_ref, h_ref, vh0, vh1, vl0, vl1,
):
    below, above, even = place("gy")
    h_ref[...] = jnp.zeros_like(h_ref)
    for k in range(REACH):
        up, down = from_sides(even, ra_ref[k], rb_ref[k])
        h_ref[:, k, :] = jnp.where(below, down, 0.0)
        h_ref[:, REACH + k, :] = jnp.where(above, up, 0.0)
    dy = dy_ref[...]

    def step(i, carry):
        for j in range(GROUP):
            z = i * GROUP + j
            sh, sl = split(sum_ref[z])
            hh, hl = split(h_ref[z])
            gy_ref[z] = rounded(dot(dy, jnp.concatenate([sh, hh, sl, hl], 0)))
        return carry

    lax.fori_loop(0, s.sz // GROUP, step, 0)
    waits = edge_planes(s)
    part = 3 * s.sy
    acc_ref[...] = jnp.zeros_like(acc_ref)
    for k in range(SPACING):
        vh, vl = ((vh0, vl0), (vh1, vl1))[k % 2]
        ready = [zc for zc in range(s.cz) if not waits[zc * SPACING + k]]
        for zc in ready:
            z = zc * SPACING + k
            for y in range(0, s.sy, 16):
                rows = slice(y, y + 16)
                grads = [r[i, rows] for r, i in ((gz_ref, z - REACH), (gy_ref, z), (gx_ref, z))]
                put_volume(s, zc * part, z, rows, diff_ref, grads, vh, vl)
        at = slice(ready[0] * part, (ready[-1] + 1) * part)
        weights = re_ref[k]
        acc_ref[at, :] += dot(
            jnp.concatenate([vh[at, :], vl[at, :]], 1), jnp.concatenate([weights, weights], 0)
        )


def edge_kernel(
    s, sum_ref, diff_ref, gx_ref, gy_ref, ra_ref, rb_ref, acc_in, ye_ref, re_ref,
    gz_ref, p_ref, za_ref, zb_ref, h_ref, vh_ref, vl_ref, acc_ref,
):
    below, above, even = place("gz")
    for k in range(REACH):
        up, down = from_sides(even, ra_ref[k], rb_ref[k])
        h_ref[k] = jnp.where(below, down, 0.0)
        h_ref[REACH + k] = jnp.where(above, up, 0.0)
    part = 3 * s.sy
    acc_ref[...] = acc_in[...]
    for side, zc in ((0, 0), (1, s.cz - 1)):
        first = 0 if side == 0 else s.sz - REACH
        for j in range(REACH):
            z = first + j
            for y in range(0, s.sy, 16):
                rows = slice(y, y + 16)

                def near(d):
                    if z + d < 0:
                        return h_ref[z + d + REACH, rows]
                    if z + d >= s.sz:
                        return h_ref[REACH + z + d - s.sz, rows]
                    return sum_ref[z + d, rows]

                gz = rounded(difference(near))
                gz_ref[side * REACH + j, rows] = gz
                row = (side * REACH + j) * part
                grads = [gz, gy_ref[z, rows], gx_ref[z, rows]]
                put_volume(s, row, z, rows, diff_ref, grads, vh_ref, vl_ref)
        lhs, rhs = [], []
        for j in range(REACH):
            row = (side * REACH + j) * part
            weights = re_ref[(first + j) % SPACING]
            for ref in (vh_ref, vl_ref):
                lhs.append(ref[row : row + part, :])
                rhs.append(weights)
        at = slice(zc * part, (zc + 1) * part)
        acc_ref[at, :] += dot(jnp.concatenate(lhs, 1), jnp.concatenate(rhs, 0))
    encode_y(s, acc_ref, ye_ref, p_ref)
    send_faces(s, p_ref, za_ref, zb_ref)


def encode_y(s, acc_ref, ye_ref, p_ref):
    columns = []
    for i in range(3 * s.cz):
        both = acc_ref[i * s.sy : (i + 1) * s.sy, :]
        columns.append(both[:, : s.tap] + both[:, s.tap :])
    high, low = split(jnp.concatenate(columns, 1))
    out = dot(ye_ref[...], jnp.concatenate([high, low, high], 0))
    for c in range(3):
        total = jnp.zeros((s.bp, s.per), F32)
        for zc in range(s.cz):
            at = (zc * 3 + c) * s.tap
            cell = out[:, at : at + s.tap]
            if s.per > s.tap:
                cell = jnp.concatenate([cell, jnp.zeros((s.bp, s.per - s.tap), F32)], 1)
            total = total + roll(cell, zc * s.cx)
        p_ref[:, c * s.per : (c + 1) * s.per] = total


def send_faces(s, p_ref, za_ref, zb_ref):
    even = place("gz")[2]
    for c in range(3):
        low = c * s.per
        down = p_ref[:, low : low + s.face]
        up = p_ref[:, low + s.own : low + s.own + s.face]
        at = slice(c * s.face, (c + 1) * s.face)
        za_ref[:, at] = jnp.where(even, up, down)
        zb_ref[:, at] = jnp.where(even, down, up)


def fold_z_kernel(s, p_ref, ra_ref, rb_ref, o_ref, ya_ref, yb_ref):
    below, above, even = place("gz")
    layer = iota((s.bp, s.per), 1) // s.cx
    first = jnp.where(below, 0, 1)
    last = jnp.where(above, s.cz + 2, s.cz)
    inside = (layer >= first) & (layer <= last)
    shared = iota((s.bp, s.face), 1) < s.used
    for c in range(3):
        low = c * s.per
        at = slice(c * s.face, (c + 1) * s.face)
        up, down = from_sides(even, ra_ref[:, at], rb_ref[:, at])
        o_ref[:, low : low + s.per] = jnp.where(inside, p_ref[:, low : low + s.per], 0.0)
        o_ref[:, low : low + s.face] += jnp.where(shared & below, down, 0.0)
        high = low + s.own
        o_ref[:, high : high + s.face] += jnp.where(shared & above, up, 0.0)
    even = place("gy")[2]
    down, up = o_ref[:8, :], o_ref[s.cy : s.cy + 8, :]
    ya_ref[...] = jnp.where(even, up, down)
    yb_ref[...] = jnp.where(even, down, up)


def fold_y(s, p_ref, ra_ref, rb_ref, v_ref):
    below, above, even = place("gy")
    up, down = from_sides(even, ra_ref[...], rb_ref[...])
    row = iota((s.bp, s.wide), 0)
    inside = (row >= jnp.where(below, 0, 1)) & (row <= jnp.where(above, s.cy + 2, s.cy))
    v_ref[...] = jnp.where(inside, p_ref[...], 0.0)
    shared = iota((8, s.wide), 0) < REACH
    v_ref[:8, :] += jnp.where(shared & below, down, 0.0)
    v_ref[s.cy : s.cy + 8, :] += jnp.where(shared & above, up, 0.0)


def own_part(s, v_ref, out_ref):
    for c in range(3):
        rows = v_ref[1 : s.cy + 1, c * s.per : (c + 1) * s.per]
        out_ref[:, c * s.own : (c + 1) * s.own] = roll(rows, -s.cx)[:, : s.own]


def operate(s, v_ref, yd_ref, rd_ref, re_ref, grads, scratch):
    even_ref, odd_ref, *pairs, acc_ref = scratch
    cells = []
    for zc in range(s.cz):
        for c in range(3):
            lanes = v_ref[:, c * s.per : (c + 1) * s.per]
            cell = roll(lanes, -zc * s.cx)[:, : s.tap]
            group = iota(cell.shape, 1) // s.cx % 2
            back = jnp.where(group == 0, roll(cell, s.cx), roll(cell, 3 * s.cx))
            cells += [cell + back, cell - back]
    ph, plow = split(jnp.concatenate(cells, 1))
    inner = dot(yd_ref[...], jnp.concatenate([ph, plow, ph], 0))
    for i in range(3 * s.cz):
        at = slice(i * s.sy, (i + 1) * s.sy)
        for j, ref in enumerate((even_ref, odd_ref)):
            low = (2 * i + j) * s.tap
            ref[at, :] = jnp.concatenate(split(inner[:, low : low + s.tap]), 1)
    gz_inner, gz_edge, gy_ref, gx_ref = grads
    square = jnp.zeros((16, s.nx), F32)
    half = SPACING // 2
    for k in range(half):
        fe_ref, fo_ref, w0, w1 = pairs[4 * (k % 2) : 4 * (k % 2) + 4]
        fe_ref[...] = dot(even_ref[...], rd_ref[k])
        fo_ref[...] = dot(odd_ref[...], rd_ref[half + k])
        for zc in range(s.cz):
            for y in range(0, s.sy, 16):
                rows = slice(y, y + 16)
                at = [
                    slice((zc * 3 + c) * s.sy + y, (zc * 3 + c) * s.sy + y + 16) for c in range(3)
                ]
                even = [fe_ref[i, :] for i in at]
                odd = [fo_ref[i, :] for i in at]
                for sign, v, w_ref in ((1, k, w0), (-1, SPACING - 1 - k, w1)):
                    z = zc * SPACING + v
                    if z < REACH:
                        gz_ref, iz = gz_edge, z
                    elif z >= s.sz - REACH:
                        gz_ref, iz = gz_edge, REACH + z - (s.sz - REACH)
                    else:
                        gz_ref, iz = gz_inner, z - REACH
                    g = [r[i, rows] for r, i in ((gz_ref, iz), (gy_ref, z), (gx_ref, z))]
                    f = [e + o if sign > 0 else e - o for e, o in zip(even, odd)]
                    dotted = g[0] * f[0] + g[1] * f[1] + g[2] * f[2]
                    square = square + dotted * dotted
                    for c in range(3):
                        w_ref[at[c], :] = (g[c] * dotted).astype(BF16)
        add = dot(
            jnp.concatenate([w0[...], w1[...]], 1),
            jnp.concatenate([re_ref[k], re_ref[SPACING - 1 - k]], 0),
        )
        acc_ref[...] = add if k == 0 else acc_ref[...] + add
    return square


def total_of(value):
    return jnp.sum(value, keepdims=True)


def moments(sums, start):
    row = iota((8, LANES), 0)
    out = jnp.zeros((8, LANES), F32)
    for k, value in enumerate(sums):
        out = jnp.where(row == start + k, value, out)
    return out


def apply_kernel(
    s, p_ref, ra_ref, rb_ref, gi_ref, ge_ref, gy_ref, gx_ref, yd_ref, rd_ref, ye_ref, re_ref,
    o_ref, za_ref, zb_ref, own_ref, sum_ref, v_ref, *scratch,
):
    fold_y(s, p_ref, ra_ref, rb_ref, v_ref)
    own_part(s, v_ref, own_ref)
    square = operate(
        s, v_ref, yd_ref, rd_ref, re_ref, (gi_ref, ge_ref, gy_ref, gx_ref), scratch
    )
    encode_y(s, scratch[-1], ye_ref, o_ref)
    send_faces(s, o_ref, za_ref, zb_ref)
    own = own_ref[...]
    sum_ref[...] = moments([total_of(own * own), total_of(square)], 0)


NEIGHBOURS = [(dz, dy) for dz in (-1, 0, 1) for dy in (-1, 0, 1) if dz or dy]


def neighbour(dz, dy):
    nz, ny = lax.axis_size("gz"), lax.axis_size("gy")
    tz, ty = lax.axis_index("gz") + dz, lax.axis_index("gy") + dy
    ok = (tz >= 0) & (tz < nz) & (ty >= 0) & (ty < ny)
    return ok, tz * ny + ty


def last_kernel(
    s, p_ref, ra_ref, rb_ref, gi_ref, ge_ref, gy_ref, gx_ref, m_ref,
    yd_ref, rd_ref, ye_ref, re_ref,
    own_ref, part_ref, send_ref, v_ref, o_ref, t_ref, y_ref, *scratch,
):
    fold_y(s, p_ref, ra_ref, rb_ref, v_ref)
    own_part(s, v_ref, own_ref)
    square = operate(
        s, v_ref, yd_ref, rd_ref, re_ref, (gi_ref, ge_ref, gy_ref, gx_ref), scratch
    )
    own = own_ref[...]
    sums = m_ref[...] + moments([total_of(own * own), total_of(square)], 2)
    encode_y(s, scratch[-1], ye_ref, o_ref)
    own_part(s, o_ref, part_ref)
    edge = s.block - LANES
    free = iota((8, LANES), 1) >= 3 * s.pair - edge
    base = jnp.where(free, sums, 0.0)
    for d in range(send_ref.shape[0]):
        send_ref[d, 0:8, edge:] = base
    lane = iota((s.bp, s.block), 1)
    t_ref[...] = jnp.zeros_like(t_ref)
    for i, dz in enumerate((-1, 1)):
        layer = 0 if dz < 0 else s.cz + 1
        width = s.cx if dz < 0 else s.pair
        total = jnp.zeros((s.bp, s.block), F32)
        for c in range(3):
            low = c * s.pair
            lanes = roll(o_ref[:, c * s.per : (c + 1) * s.per], low - layer * s.cx)
            total = jnp.where((lane >= low) & (lane < low + width), lanes[:, : s.block], total)
        t_ref[i, 8 : 8 + s.bp, :] = total
    for c in range(3):
        lanes = roll(o_ref[:, c * s.per : (c + 1) * s.per], -s.cx)
        y_ref[:, c * s.own : (c + 1) * s.own] = lanes[:, : s.own]
    for dz, dy in NEIGHBOURS:
        ok, target = neighbour(dz, dy)

        @pl.when(ok)
        def _(dz=dz, dy=dy, target=target):
            if dz:
                start = {-1: 9 - s.cy, 0: 9, 1: 9 + s.cy}[dy]
                rows = t_ref[(dz + 1) // 2, start : start + 8, :]
                send_ref[target, 0:8, :edge] = rows[:, :edge]
                send_ref[target, 0:8, edge:] = jnp.where(free, sums, rows[:, edge:])
            else:
                for c in range(3):
                    lanes = slice(c * s.own, (c + 1) * s.own)
                    if dy > 0:
                        send_ref[target, 2 * c : 2 * c + 2, : s.own] = y_ref[
                            s.cy + 1 : s.cy + 3, lanes
                        ]
                    else:
                        send_ref[target, c : c + 1, : s.own] = y_ref[0:1, lanes]


def finish_kernel(s, v0_ref, v1_ref, part_ref, got_ref, u_ref, r_ref, v_ref, t_ref):
    v_ref[...] = part_ref[...]
    for i, dz in enumerate((-1, 1)):
        t_ref[i] = jnp.zeros((8, s.block), F32)
        for dy in (-1, 0, 1):
            ok, source = neighbour(dz, dy)

            @pl.when(ok)
            def _(i=i, source=source):
                t_ref[i] += got_ref[source]

    lane = iota((8, s.own), 1)
    for c in range(3):
        low = c * s.pair
        lanes = slice(c * s.own, (c + 1) * s.own)
        first = roll(t_ref[0], -low)[:, : s.own]
        last = roll(t_ref[1], (s.cz - 1) * s.cx - low)[:, : s.own]
        v_ref[:, lanes] += jnp.where(lane < s.pair, first, 0.0)
        v_ref[:, lanes] += jnp.where(lane >= s.own - s.cx, last, 0.0)
    for dy in (-1, 1):
        ok, source = neighbour(0, dy)

        @pl.when(ok)
        def _(dy=dy, source=source):
            for c in range(3):
                lanes = slice(c * s.own, (c + 1) * s.own)
                if dy < 0:
                    v_ref[0:2, lanes] += got_ref[source, 2 * c : 2 * c + 2, : s.own]
                else:
                    v_ref[s.cy - 1 : s.cy, lanes] += got_ref[source, c : c + 1, : s.own]

    edge = s.block - LANES
    tot = got_ref[0, :, edge:]
    for d in range(1, got_ref.shape[0]):
        tot = tot + got_ref[d, :, edge:]
    m0, m1, m2, m3 = (tot[k : k + 1, LANES - 1 : LANES] for k in range(4))
    v0, v1, v2 = v0_ref[...], v1_ref[...], v_ref[...]
    rho = m1 / m0
    a0 = 1.0 / (rho + DAMPING)
    rr1 = a0 * a0 * (m2 - rho * m1)
    beta = rr1 / m0
    quad = a0 * a0 * (m3 - 2.0 * rho * m2 + rho * rho * m1) + DAMPING * rr1
    a1 = rr1 / (quad - beta * rr1 / a0)
    r1 = a0 * (rho * v0 - v1)
    image = a0 * (rho * v1 - v2) + DAMPING * r1 + beta * (v1 + DAMPING * v0)
    update = a0 * v0 + a1 * (r1 + beta * v0)
    residual = r1 - a1 * image
    for out_ref, value in ((u_ref, update), (r_ref, residual)):
        for c in range(3):
            for a in range(s.cz):
                at = c * s.own + a * s.cx
                out_ref[c, a] = value[:, at : at + s.cx]


def swap(value_a, value_b, axis):
    count = lax.axis_size(axis)
    even = [(i, i ^ 1) for i in range(count)]
    odd = [(i, (i + (1 if i % 2 else -1)) % count) for i in range(count)]
    return lax.ppermute(value_a, axis, even), lax.ppermute(value_b, axis, odd)


def scratch_of(item):
    if not isinstance(item, tuple):
        return item
    return pltpu.VMEM(*(item if isinstance(item[0], tuple) else (item, F32)))


def call(kernel, name, outs, scratch, *args, far=0):
    shapes = [jax.ShapeDtypeStruct(o, F32) for o in outs]
    return pl.pallas_call(
        kernel,
        out_shape=shapes,
        in_specs=[HBM] * far + [VMEM] * (len(args) - far),
        out_specs=[VMEM] * len(outs),
        scratch_shapes=[scratch_of(n) for n in scratch],
        compiler_params=PARAMS,
        name=name,
    )(*[pltpu.with_memory_space_constraint(v, pltpu.HBM) for v in args[:far]], *args[far:])


def shards(fixed, moving):
    s = Sizes(fixed.shape)
    devices = lax.axis_size("gz") * lax.axis_size("gy")
    dx, dy = gradient_consts(s)
    yd, rd, ye, re = consts(s)
    part = functools.partial

    zhalo, yhalo = (REACH, s.sy, s.nx), (REACH, s.sz, s.nx)
    za, zb = call(
        part(faces_z_kernel, s),
        "faces_z",
        [zhalo, zhalo],
        [(2, 2, *zhalo), pltpu.SemaphoreType.DMA((2, 2))],
        fixed, moving, far=2,
    )
    za, zb = swap(za, zb, "gz")
    ya, yb = call(part(faces_y_kernel, s), "faces_y", [yhalo, yhalo], [], fixed, moving)
    ya, yb = swap(ya, yb, "gy")
    volume = fixed.shape
    total, diff, gx, gz_inner = call(
        part(start_kernel, s),
        "start",
        [volume, volume, volume, (s.sz - 2 * REACH, s.sy, s.nx)],
        [],
        fixed, moving, dx,
    )
    acc = (s.cells, 2 * s.tap)
    half = ((s.cells, s.nx), BF16)
    gy, inner = call(
        part(inner_kernel, s),
        "inner",
        [volume, acc],
        [(s.sz, 16, s.nx), half, half, half, half],
        total, diff, gx, gz_inner, ya, yb, dy, re,
    )
    grid, zface, yface = (s.bp, s.wide), (s.bp, 3 * s.face), (8, s.wide)
    few = ((2 * REACH * 3 * s.sy, s.nx), BF16)
    gz_edge, grid0, za, zb = call(
        part(edge_kernel, s),
        "edge",
        [(2 * REACH, s.sy, s.nx), grid, zface, zface],
        [(2 * REACH, s.sy, s.nx), few, few, acc],
        total, diff, gx, gy, za, zb, inner, ye, re,
    )

    def fold_z(value, za, zb):
        za, zb = swap(za, zb, "gz")
        value, ya, yb = call(
            part(fold_z_kernel, s), "fold_z", [grid, yface, yface], [], value, za, zb
        )
        return (value, *swap(ya, yb, "gy"))

    own = (s.cy, 3 * s.own)
    field = (s.cells, s.nx)
    left = ((s.cells, 2 * s.tap), BF16)
    work = [left, left, *[field, field, half, half] * 2, acc]
    grads = (gz_inner, gz_edge, gy, gx)
    grid1, za, zb, v0, sums = call(
        part(apply_kernel, s),
        "apply",
        [grid, zface, zface, own, (8, LANES)],
        [grid, *work],
        *fold_z(grid0, za, zb), *grads, yd, rd, ye, re,
    )
    v1, mine, send = call(
        part(last_kernel, s),
        "last",
        [own, own, (devices, s.cy, s.block)],
        [grid, grid, (2, 16 + s.bp, s.block), (s.bp, 3 * s.own), *work],
        *fold_z(grid1, za, zb), *grads, sums, yd, rd, ye, re,
    )
    got = lax.all_to_all(send, ("gz", "gy"), 0, 0)
    out = (3, s.cz, s.cy, s.cx)
    return tuple(
        call(
            part(finish_kernel, s), "finish", [out, out], [own, (2, s.cy, s.block)], v0, v1, mine, got
        )
    )


def solution(mesh):
    return jax.shard_map(
        shards,
        mesh=mesh,
        in_specs=(P("gz", "gy", None), P("gz", "gy", None)),
        out_specs=(P(None, "gz", "gy", None), P(None, "gz", "gy", None)),
        check_vma=False,
    )
```

```python
import functools

import jax
import jax.numpy as jnp
import numpy as np
from jax import lax
from jax.experimental import pallas as pl
from jax.experimental.pallas import tpu as pltpu
from jax.sharding import PartitionSpec as P

SPACING = 8
DAMPING = 8.0
LANES = 128
REACH = 3
F32 = jnp.float32
BF16 = jnp.bfloat16
VMEM = pl.BlockSpec(memory_space=pltpu.VMEM)
HBM = pl.BlockSpec(memory_space=pltpu.MemorySpace.HBM)
PARAMS = pltpu.CompilerParams(vmem_limit_bytes=20 * 1024 * 1024)


def round_up(value, step):
    return -(-value // step) * step


class Sizes:
    def __init__(self, shape):
        self.sz, self.sy, self.nx = shape
        self.cz, self.cy, self.cx = (n // SPACING for n in shape)
        self.na, self.nb = self.cz + 3, self.cy + 3
        self.bp = round_up(self.nb, 16)
        self.per = round_up(self.na * self.cx, LANES)
        self.wide = 3 * self.per
        self.tap = 4 * self.cx
        self.face = round_up(REACH * self.cx, LANES)
        self.used = REACH * self.cx
        self.own = self.cz * self.cx
        self.cells = 3 * self.cz * self.sy
        self.pair = 2 * self.cx
        assert 2 * 3 * self.pair == 3 * LANES and self.own == LANES
        self.block = self.cy + self.cy // 2 + 1
        assert self.tap % LANES == 0 and self.own % LANES == 0
        assert self.cy % 8 == 0 and self.bp == self.cy + 8 and self.cz > 1


def taps():
    t = (np.arange(SPACING) + 0.5) / SPACING
    return np.stack(
        [
            (1 - t) ** 3 / 6,
            (3 * t**3 - 6 * t**2 + 4) / 6,
            (-3 * t**3 + 3 * t**2 + 3 * t + 1) / 6,
            t**3 / 6,
        ]
    )


def basis(count, columns, offset):
    w = taps()
    out = np.zeros((count, columns))
    for v in range(count):
        for k in range(4):
            col = v // SPACING - 1 + k + offset
            if 0 <= col < columns:
                out[v, col] += w[k, v % SPACING]
    return out


def halves(matrix):
    high = np.asarray(matrix, np.float32).astype(jnp.bfloat16)
    low = (matrix - high.astype(np.float64)).astype(np.float32).astype(jnp.bfloat16)
    return high, low


def consts(s):
    by = basis(s.sy, s.bp, 1)
    yh, yl = halves(by)
    y_decode = np.concatenate([yh, yh, yl], 1)
    y_encode = np.concatenate([yh.T, yh.T, yl.T], 1)
    bx = basis(s.nx, s.cx, 0)
    w = taps()
    decode, encode = [], []
    for k in range(SPACING):
        high, low = halves(np.concatenate([w[t, k] * bx.T for t in range(4)], 0))
        encode.append(np.concatenate([high.T, low.T], 1))
    for sign in (1.0, -1.0):
        for k in range(SPACING // 2):
            parts = [0.5 * (w[t, k] + sign * w[3 - t, k]) * bx.T for t in range(2)]
            (h0, l0), (h1, l1) = (halves(v) for v in parts)
            flip = np.asarray(sign, jnp.bfloat16)
            zero = np.zeros((2 * s.cx, s.nx), jnp.bfloat16)
            decode.append(np.concatenate([h0, h1, flip * l1, flip * l0, h0, h1, zero], 0))
    return tuple(jnp.asarray(v) for v in (y_decode, np.stack(decode), y_encode, np.stack(encode)))


def gradient_consts(s):
    coef = {-3: -1.0, -2: 9.0, -1: -45.0, 1: 45.0, 2: -9.0, 3: 1.0}
    dx = np.zeros((s.nx, s.nx))
    for x in range(s.nx):
        for d, value in coef.items():
            if 0 <= x + d < s.nx:
                dx[x + d, x] = value
    dy = np.zeros((s.sy, s.sy + 16))
    for y in range(s.sy):
        for d, value in coef.items():
            at = y + d
            if at < 0:
                dy[y, s.sy + REACH + at] = value
            elif at >= s.sy:
                dy[y, s.sy + REACH + at - s.sy] = value
            else:
                dy[y, at] = value
    dx, dy = (v.astype(jnp.bfloat16) for v in (dx, dy))
    return jnp.asarray(np.concatenate([dx, dx], 0)), jnp.asarray(np.concatenate([dy, dy], 1))


def split(value):
    high = value.astype(BF16)
    return high, (value - high.astype(F32)).astype(BF16)


def dot(a, b):
    return jnp.dot(a, b, preferred_element_type=F32)


def rounded(value):
    return (value * F32(1.0 / 120.0)).astype(BF16).astype(F32)


def place(axis):
    index = lax.axis_index(axis)
    count = lax.axis_size(axis)
    return index > 0, index < count - 1, lax.rem(index, 2) == 0


def from_sides(even, a, b):
    return jnp.where(even, a, b), jnp.where(even, b, a)


def difference(near):
    return (
        45.0 * (near(1) - near(-1)) - 9.0 * (near(2) - near(-2)) + (near(3) - near(-3))
    )


def iota(shape, dim):
    return lax.broadcasted_iota(jnp.int32, shape, dim)


def roll(value, shift):
    shift = shift % value.shape[1]
    return pltpu.roll(value, shift, 1) if shift else value


def start_all(copies):
    for copy in copies:
        copy.start()
    return copies


def faces_z_kernel(s, f_ref, m_ref, za_ref, zb_ref, t_ref, sems):
    copies = []
    for i, ref in enumerate((f_ref, m_ref)):
        for j in range(2):
            z = pl.ds(j * (s.sz - REACH), REACH)
            copies.append(pltpu.make_async_copy(ref.at[z], t_ref.at[i, j], sems.at[i, j]))
    for copy in start_all(copies):
        copy.wait()
    even = place("gz")[2]
    down, up = (t_ref[0, j] + t_ref[1, j] for j in range(2))
    za_ref[...] = jnp.where(even, up, down)
    zb_ref[...] = jnp.where(even, down, up)


def faces_y_kernel(s, f_ref, m_ref, ya_ref, yb_ref):
    even = place("gy")[2]
    for k in range(REACH):
        high = s.sy - REACH + k
        down = f_ref[:, k, :] + m_ref[:, k, :]
        up = f_ref[:, high, :] + m_ref[:, high, :]
        ya_ref[k] = jnp.where(even, up, down)
        yb_ref[k] = jnp.where(even, down, up)


GROUP = 4


def start_kernel(s, f_ref, m_ref, dx_ref, sum_ref, diff_ref, gx_ref, gz_ref):
    dx = dx_ref[...]
    for i in range(s.sz // GROUP):
        planes = slice(i * GROUP, (i + 1) * GROUP)
        f, m = f_ref[planes], m_ref[planes]
        total = f + m
        sum_ref[planes] = total
        diff_ref[planes] = f - m
        sh, sl = split(total.reshape(GROUP * s.sy, s.nx))
        gx = rounded(dot(jnp.concatenate([sh, sl], 1), dx))
        gx_ref[planes] = gx.reshape(GROUP, s.sy, s.nx)

    def step(i, carry):
        for y in range(0, s.sy, 16):
            rows = slice(y, y + 16)
            gz_ref[i, rows] = rounded(difference(lambda d: sum_ref[i + REACH + d, rows]))
        return carry

    lax.fori_loop(0, s.sz - 2 * REACH, step, 0)


def edge_planes(s):
    return [z < REACH or z >= s.sz - REACH for z in range(s.sz)]


def put_volume(s, row, z, rows, diff_ref, grads, high_ref, low_ref):
    mm = diff_ref[z, rows]
    for c in range(3):
        high, low = split(mm * grads[c])
        at = slice(row + c * s.sy + rows.start, row + c * s.sy + rows.stop)
        high_ref[at, :] = high
        low_ref[at, :] = low


def inner_kernel(
    s, sum_ref, diff_ref, gx_ref, gz_ref, ra_ref, rb_ref, dy_ref, re_ref,
    gy_ref, acc_ref, h_ref, vh0, vh1, vl0, vl1,
):
    below, above, even = place("gy")
    h_ref[...] = jnp.zeros_like(h_ref)
    for k in range(REACH):
        up, down = from_sides(even, ra_ref[k], rb_ref[k])
        h_ref[:, k, :] = jnp.where(below, down, 0.0)
        h_ref[:, REACH + k, :] = jnp.where(above, up, 0.0)
    dy = dy_ref[...]

    def step(i, carry):
        for j in range(GROUP):
            z = i * GROUP + j
            sh, sl = split(sum_ref[z])
            hh, hl = split(h_ref[z])
            gy_ref[z] = rounded(dot(dy, jnp.concatenate([sh, hh, sl, hl], 0)))
        return carry

    lax.fori_loop(0, s.sz // GROUP, step, 0)
    waits = edge_planes(s)
    part = 3 * s.sy
    acc_ref[...] = jnp.zeros_like(acc_ref)
    for k in range(SPACING):
        vh, vl = ((vh0, vl0), (vh1, vl1))[k % 2]
        ready = [zc for zc in range(s.cz) if not waits[zc * SPACING + k]]
        for zc in ready:
            z = zc * SPACING + k
            for y in range(0, s.sy, 16):
                rows = slice(y, y + 16)
                grads = [r[i, rows] for r, i in ((gz_ref, z - REACH), (gy_ref, z), (gx_ref, z))]
                put_volume(s, zc * part, z, rows, diff_ref, grads, vh, vl)
        at = slice(ready[0] * part, (ready[-1] + 1) * part)
        weights = re_ref[k]
        acc_ref[at, :] += dot(
            jnp.concatenate([vh[at, :], vl[at, :]], 1), jnp.concatenate([weights, weights], 0)
        )


def edge_kernel(
    s, sum_ref, diff_ref, gx_ref, gy_ref, ra_ref, rb_ref, acc_in, ye_ref, re_ref,
    gz_ref, p_ref, za_ref, zb_ref, h_ref, vh_ref, vl_ref, acc_ref,
):
    below, above, even = place("gz")
    for k in range(REACH):
        up, down = from_sides(even, ra_ref[k], rb_ref[k])
        h_ref[k] = jnp.where(below, down, 0.0)
        h_ref[REACH + k] = jnp.where(above, up, 0.0)
    part = 3 * s.sy
    for side, zc in ((0, 0), (1, s.cz - 1)):
        first = 0 if side == 0 else s.sz - REACH
        for j in range(REACH):
            z = first + j
            for y in range(0, s.sy, 16):
                rows = slice(y, y + 16)

                def near(d):
                    if z + d < 0:
                        return h_ref[z + d + REACH, rows]
                    if z + d >= s.sz:
                        return h_ref[REACH + z + d - s.sz, rows]
                    return sum_ref[z + d, rows]

                gz = rounded(difference(near))
                gz_ref[side * REACH + j, rows] = gz
                row = (side * REACH + j) * part
                grads = [gz, gy_ref[z, rows], gx_ref[z, rows]]
                put_volume(s, row, z, rows, diff_ref, grads, vh_ref, vl_ref)
        lhs, rhs = [], []
        for j in range(REACH):
            row = (side * REACH + j) * part
            weights = re_ref[(first + j) % SPACING]
            for ref in (vh_ref, vl_ref):
                lhs.append(ref[row : row + part, :])
                rhs.append(weights)
        at = slice(zc * part, (zc + 1) * part)
        acc_ref[at, :] = acc_in[at, :] + dot(jnp.concatenate(lhs, 1), jnp.concatenate(rhs, 0))
    encode_y(s, [acc_ref] + [acc_in] * (s.cz - 2) + [acc_ref], ye_ref, p_ref)
    send_faces(s, p_ref, za_ref, zb_ref)


def encode_y(s, acc_refs, ye_ref, p_ref):
    columns = []
    for i in range(3 * s.cz):
        both = acc_refs[i // 3][i * s.sy : (i + 1) * s.sy, :]
        columns.append(both[:, : s.tap] + both[:, s.tap :])
    high, low = split(jnp.concatenate(columns, 1))
    out = dot(ye_ref[...], jnp.concatenate([high, low, high], 0))
    for c in range(3):
        total = jnp.zeros((s.bp, s.per), F32)
        for zc in range(s.cz):
            at = (zc * 3 + c) * s.tap
            cell = out[:, at : at + s.tap]
            if s.per > s.tap:
                cell = jnp.concatenate([cell, jnp.zeros((s.bp, s.per - s.tap), F32)], 1)
            total = total + roll(cell, zc * s.cx)
        p_ref[:, c * s.per : (c + 1) * s.per] = total


def send_faces(s, p_ref, za_ref, zb_ref):
    even = place("gz")[2]
    for c in range(3):
        low = c * s.per
        down = p_ref[:, low : low + s.face]
        up = p_ref[:, low + s.own : low + s.own + s.face]
        at = slice(c * s.face, (c + 1) * s.face)
        to_a, to_b = jnp.where(even, up, down), jnp.where(even, down, up)
        for i in range(za_ref.shape[0]):
            za_ref[i, :, at] = to_a[4 * i : 4 * i + 4]
            zb_ref[i, :, at] = to_b[4 * i : 4 * i + 4]


def fold_z_kernel(s, p_ref, ra_ref, rb_ref, o_ref, ya_ref, yb_ref):
    below, above, even = place("gz")
    layer = iota((s.bp, s.per), 1) // s.cx
    first = jnp.where(below, 0, 1)
    last = jnp.where(above, s.cz + 2, s.cz)
    inside = (layer >= first) & (layer <= last)
    shared = iota((4, s.face), 1) < s.used
    for c in range(3):
        low = c * s.per
        high = low + s.own
        at = slice(c * s.face, (c + 1) * s.face)
        o_ref[:, low : low + s.per] = jnp.where(inside, p_ref[:, low : low + s.per], 0.0)
        for i in range(ra_ref.shape[0]):
            rows = slice(4 * i, 4 * i + 4)
            up, down = from_sides(even, ra_ref[i, :, at], rb_ref[i, :, at])
            o_ref[rows, low : low + s.face] += jnp.where(shared & below, down, 0.0)
            o_ref[rows, high : high + s.face] += jnp.where(shared & above, up, 0.0)
    even = place("gy")[2]
    down, up = o_ref[:4, :], o_ref[s.cy : s.cy + 4, :]
    ya_ref[...] = jnp.where(even, up, down)
    yb_ref[...] = jnp.where(even, down, up)


def fold_y(s, p_ref, ra_ref, rb_ref, v_ref):
    below, above, even = place("gy")
    up, down = from_sides(even, ra_ref[...], rb_ref[...])
    row = iota((s.bp, s.wide), 0)
    inside = (row >= jnp.where(below, 0, 1)) & (row <= jnp.where(above, s.cy + 2, s.cy))
    v_ref[...] = jnp.where(inside, p_ref[...], 0.0)
    shared = iota((4, s.wide), 0) < REACH
    v_ref[:4, :] += jnp.where(shared & below, down, 0.0)
    v_ref[s.cy : s.cy + 4, :] += jnp.where(shared & above, up, 0.0)


def own_part(s, v_ref, out_ref):
    for c in range(3):
        rows = v_ref[1 : s.cy + 1, c * s.per : (c + 1) * s.per]
        out_ref[:, c * s.own : (c + 1) * s.own] = roll(rows, -s.cx)[:, : s.own]


def operate(s, v_ref, yd_ref, rd_ref, re_ref, grads, scratch):
    even_ref, odd_ref, *pairs, acc_ref = scratch
    cells = []
    for zc in range(s.cz):
        for c in range(3):
            lanes = v_ref[:, c * s.per : (c + 1) * s.per]
            cell = roll(lanes, -zc * s.cx)[:, : s.tap]
            group = iota(cell.shape, 1) // s.cx % 2
            back = jnp.where(group == 0, roll(cell, s.cx), roll(cell, 3 * s.cx))
            cells += [cell + back, cell - back]
    ph, plow = split(jnp.concatenate(cells, 1))
    inner = dot(yd_ref[...], jnp.concatenate([ph, plow, ph], 0))
    for i in range(3 * s.cz):
        at = slice(i * s.sy, (i + 1) * s.sy)
        for j, ref in enumerate((even_ref, odd_ref)):
            low = (2 * i + j) * s.tap
            ref[at, :] = jnp.concatenate(split(inner[:, low : low + s.tap]), 1)
    gz_inner, gz_edge, gy_ref, gx_ref = grads
    square = jnp.zeros((16, s.nx), F32)
    half = SPACING // 2
    for k in range(half):
        fe_ref, fo_ref, w0, w1 = pairs[4 * (k % 2) : 4 * (k % 2) + 4]
        fe_ref[...] = dot(even_ref[...], rd_ref[k])
        fo_ref[...] = dot(odd_ref[...], rd_ref[half + k])
        for zc in range(s.cz):
            for y in range(0, s.sy, 16):
                rows = slice(y, y + 16)
                at = [
                    slice((zc * 3 + c) * s.sy + y, (zc * 3 + c) * s.sy + y + 16) for c in range(3)
                ]
                even = [fe_ref[i, :] for i in at]
                odd = [fo_ref[i, :] for i in at]
                for sign, v, w_ref in ((1, k, w0), (-1, SPACING - 1 - k, w1)):
                    z = zc * SPACING + v
                    if z < REACH:
                        gz_ref, iz = gz_edge, z
                    elif z >= s.sz - REACH:
                        gz_ref, iz = gz_edge, REACH + z - (s.sz - REACH)
                    else:
                        gz_ref, iz = gz_inner, z - REACH
                    g = [r[i, rows] for r, i in ((gz_ref, iz), (gy_ref, z), (gx_ref, z))]
                    f = [e + o if sign > 0 else e - o for e, o in zip(even, odd)]
                    dotted = g[0] * f[0] + g[1] * f[1] + g[2] * f[2]
                    square = square + dotted * dotted
                    for c in range(3):
                        w_ref[at[c], :] = (g[c] * dotted).astype(BF16)
        add = dot(
            jnp.concatenate([w0[...], w1[...]], 1),
            jnp.concatenate([re_ref[k], re_ref[SPACING - 1 - k]], 0),
        )
        acc_ref[...] = add if k == 0 else acc_ref[...] + add
    return square


def total_of(value):
    return jnp.sum(value, keepdims=True)


def moments(sums, start):
    lane = iota((1, LANES), 1)
    out = jnp.zeros((1, LANES), F32)
    for k, value in enumerate(sums):
        out = jnp.where(lane == start + k, value, out)
    return out


def apply_kernel(
    s, p_ref, ra_ref, rb_ref, gi_ref, ge_ref, gy_ref, gx_ref, yd_ref, rd_ref, ye_ref, re_ref,
    o_ref, za_ref, zb_ref, own_ref, sum_ref, v_ref, *scratch,
):
    fold_y(s, p_ref, ra_ref, rb_ref, v_ref)
    own_part(s, v_ref, own_ref)
    square = operate(
        s, v_ref, yd_ref, rd_ref, re_ref, (gi_ref, ge_ref, gy_ref, gx_ref), scratch
    )
    encode_y(s, [scratch[-1]] * s.cz, ye_ref, o_ref)
    send_faces(s, o_ref, za_ref, zb_ref)
    own = own_ref[...]
    sum_ref[...] = moments([total_of(own * own), total_of(square)], 0)


NEIGHBOURS = [(dz, dy) for dz in (-1, 0, 1) for dy in (-1, 0, 1) if dz or dy]


def neighbour(dz, dy):
    nz, ny = lax.axis_size("gz"), lax.axis_size("gy")
    iz, iy = lax.axis_index("gz"), lax.axis_index("gy")
    tz, ty = iz + dz, iy + dy
    ok = (tz >= 0) & (tz < nz) & (ty >= 0) & (ty < ny)
    return ok, jnp.where(ok, tz * ny + ty, iz * ny + iy)


def last_kernel(
    s, p_ref, ra_ref, rb_ref, gi_ref, ge_ref, gy_ref, gx_ref, m_ref,
    yd_ref, rd_ref, ye_ref, re_ref,
    own_ref, part_ref, send_ref, v_ref, o_ref, t_ref, y_ref, *scratch,
):
    fold_y(s, p_ref, ra_ref, rb_ref, v_ref)
    own_part(s, v_ref, own_ref)
    square = operate(
        s, v_ref, yd_ref, rd_ref, re_ref, (gi_ref, ge_ref, gy_ref, gx_ref), scratch
    )
    own = own_ref[...]
    sums = m_ref[...] + moments([total_of(own * own), total_of(square)], 2)
    encode_y(s, [scratch[-1]] * s.cz, ye_ref, o_ref)
    own_part(s, o_ref, part_ref)
    for d in range(send_ref.shape[0]):
        send_ref[d, s.block - 1, :, :] = sums
    lane = iota((s.bp, 2 * LANES), 1)
    t_ref[...] = jnp.zeros_like(t_ref)
    for i, dz in enumerate((-1, 1)):
        layer = 0 if dz < 0 else s.cz + 1
        width = s.cx if dz < 0 else s.pair
        total = jnp.zeros((s.bp, 2 * LANES), F32)
        for c in range(3):
            low = c * s.pair
            lanes = roll(o_ref[:, c * s.per : (c + 1) * s.per], low - layer * s.cx)
            total = jnp.where((lane >= low) & (lane < low + width), lanes[:, : 2 * LANES], total)
        t_ref[i, 8 : 8 + s.bp, :] = total
    for c in range(3):
        lanes = roll(o_ref[:, c * s.per : (c + 1) * s.per], -s.cx)
        y_ref[:, c * s.own : (c + 1) * s.own] = lanes[:, : s.own]
    half = s.cy // 2
    low_half = iota((half, LANES), 1) < LANES // 2
    for dz, dy in NEIGHBOURS:
        _, target = neighbour(dz, dy)
        if dz:
            start = 9 + dy * s.cy
            side = (dz + 1) // 2
            send_ref[target, 0 : s.cy, 0, :] = t_ref[side, start : start + s.cy, :LANES]
            near = t_ref[side, start : start + half, LANES:]
            far = t_ref[side, start + half : start + s.cy, LANES:]
            send_ref[target, s.cy : s.cy + half, 0, :] = jnp.where(
                low_half, near, roll(far, LANES // 2)
            )
        else:
            for c in range(3):
                lanes = slice(c * s.own, (c + 1) * s.own)
                if dy > 0:
                    send_ref[target, 2 * c : 2 * c + 2, 0, :] = y_ref[s.cy + 1 : s.cy + 3, lanes]
                else:
                    send_ref[target, c, :, :] = y_ref[0:1, lanes]


def finish_kernel(s, v0_ref, v1_ref, part_ref, got_ref, u_ref, r_ref, v_ref, t_ref, w_ref):
    v_ref[...] = part_ref[...]
    half = s.cy // 2
    for i, dz in enumerate((-1, 1)):
        first = jnp.zeros((s.cy, LANES), F32)
        rest = jnp.zeros((half, LANES), F32)
        for dy in (-1, 0, 1):
            ok, source = neighbour(dz, dy)
            first += jnp.where(ok, got_ref[source, 0 : s.cy, 0, :], 0.0)
            rest += jnp.where(ok, got_ref[source, s.cy : s.cy + half, 0, :], 0.0)
        t_ref[i] = first
        w_ref[i, 0:half, :] = rest
        w_ref[i, half:, :] = roll(rest, LANES // 2)

    lane = iota((s.cy, s.own), 1)
    for c in range(3):
        lanes = slice(c * s.own, (c + 1) * s.own)
        first, last = (w_ref[0], w_ref[1]) if c == 2 else (t_ref[0], t_ref[1])
        low = c % 2 * s.pair
        v_ref[:, lanes] += jnp.where(lane < s.pair, roll(first, -low), 0.0)
        last = roll(last, (s.cz - 1) * s.cx - low)
        v_ref[:, lanes] += jnp.where(lane >= s.own - s.cx, last, 0.0)
    for dy in (-1, 1):
        ok, source = neighbour(0, dy)
        for c in range(3):
            lanes = slice(c * s.own, (c + 1) * s.own)
            if dy < 0:
                value = got_ref[source, 2 * c : 2 * c + 2, 0, :]
                v_ref[0:2, lanes] += jnp.where(ok, value, 0.0)
            else:
                v_ref[s.cy - 1 : s.cy, lanes] += jnp.where(ok, got_ref[source, c, :, :], 0.0)

    tot = jnp.sum(got_ref[:, s.block - 1, 0, :], axis=0, keepdims=True)
    m0, m1, m2, m3 = (tot[:, k : k + 1] for k in range(4))
    v0, v1, v2 = v0_ref[...], v1_ref[...], v_ref[...]
    rho = m1 / m0
    a0 = 1.0 / (rho + DAMPING)
    rr1 = a0 * a0 * (m2 - rho * m1)
    beta = rr1 / m0
    quad = a0 * a0 * (m3 - 2.0 * rho * m2 + rho * rho * m1) + DAMPING * rr1
    a1 = rr1 / (quad - beta * rr1 / a0)
    r1 = a0 * (rho * v0 - v1)
    image = a0 * (rho * v1 - v2) + DAMPING * r1 + beta * (v1 + DAMPING * v0)
    update = a0 * v0 + a1 * (r1 + beta * v0)
    residual = r1 - a1 * image
    for out_ref, value in ((u_ref, update), (r_ref, residual)):
        for c in range(3):
            for a in range(s.cz):
                at = c * s.own + a * s.cx
                out_ref[c, a] = value[:, at : at + s.cx]


def swap(value_a, value_b, axis):
    count = lax.axis_size(axis)
    even = [(i, i ^ 1) for i in range(count)]
    odd = [(i, (i + (1 if i % 2 else -1)) % count) for i in range(count)]
    return lax.ppermute(value_a, axis, even), lax.ppermute(value_b, axis, odd)


def scratch_of(item):
    if not isinstance(item, tuple):
        return item
    return pltpu.VMEM(*(item if isinstance(item[0], tuple) else (item, F32)))


def call(kernel, name, outs, scratch, *args, far=0):
    shapes = [jax.ShapeDtypeStruct(o, F32) for o in outs]
    return pl.pallas_call(
        kernel,
        out_shape=shapes,
        in_specs=[HBM] * far + [VMEM] * (len(args) - far),
        out_specs=[VMEM] * len(outs),
        scratch_shapes=[scratch_of(n) for n in scratch],
        compiler_params=PARAMS,
        name=name,
    )(*[pltpu.with_memory_space_constraint(v, pltpu.HBM) for v in args[:far]], *args[far:])


def shards(fixed, moving):
    s = Sizes(fixed.shape)
    devices = lax.axis_size("gz") * lax.axis_size("gy")
    dx, dy = gradient_consts(s)
    yd, rd, ye, re = consts(s)
    part = functools.partial

    zhalo, yhalo = (REACH, s.sy, s.nx), (REACH, s.sz, s.nx)
    za, zb = call(
        part(faces_z_kernel, s),
        "faces_z",
        [zhalo, zhalo],
        [(2, 2, *zhalo), pltpu.SemaphoreType.DMA((2, 2))],
        fixed, moving, far=2,
    )
    za, zb = swap(za, zb, "gz")
    ya, yb = call(part(faces_y_kernel, s), "faces_y", [yhalo, yhalo], [], fixed, moving)
    ya, yb = swap(ya, yb, "gy")
    volume = fixed.shape
    total, diff, gx, gz_inner = call(
        part(start_kernel, s),
        "start",
        [volume, volume, volume, (s.sz - 2 * REACH, s.sy, s.nx)],
        [],
        fixed, moving, dx,
    )
    acc = (s.cells, 2 * s.tap)
    half = ((s.cells, s.nx), BF16)
    gy, inner = call(
        part(inner_kernel, s),
        "inner",
        [volume, acc],
        [(s.sz, 16, s.nx), half, half, half, half],
        total, diff, gx, gz_inner, ya, yb, dy, re,
    )
    grid, zface, yface = (s.bp, s.wide), (round_up(s.nb, 4) // 4, 4, 3 * s.face), (4, s.wide)
    few = ((2 * REACH * 3 * s.sy, s.nx), BF16)
    gz_edge, grid0, za, zb = call(
        part(edge_kernel, s),
        "edge",
        [(2 * REACH, s.sy, s.nx), grid, zface, zface],
        [(2 * REACH, s.sy, s.nx), few, few, acc],
        total, diff, gx, gy, za, zb, inner, ye, re,
    )

    def fold_z(value, za, zb):
        za, zb = swap(za, zb, "gz")
        value, ya, yb = call(
            part(fold_z_kernel, s), "fold_z", [grid, yface, yface], [], value, za, zb
        )
        return (value, *swap(ya, yb, "gy"))

    own = (s.cy, 3 * s.own)
    field = (s.cells, s.nx)
    left = ((s.cells, 2 * s.tap), BF16)
    work = [left, left, *[field, field, half, half] * 2, acc]
    grads = (gz_inner, gz_edge, gy, gx)
    grid1, za, zb, v0, sums = call(
        part(apply_kernel, s),
        "apply",
        [grid, zface, zface, own, (1, LANES)],
        [grid, *work],
        *fold_z(grid0, za, zb), *grads, yd, rd, ye, re,
    )
    v1, mine, send = call(
        part(last_kernel, s),
        "last",
        [own, own, (devices, s.block, 1, LANES)],
        [grid, grid, (2, 16 + s.bp, 2 * LANES), (s.bp, 3 * s.own), *work],
        *fold_z(grid1, za, zb), *grads, sums, yd, rd, ye, re,
    )
    got = lax.all_to_all(send, ("gz", "gy"), 0, 0)
    out = (3, s.cz, s.cy, s.cx)
    return tuple(
        call(
            part(finish_kernel, s), "finish", [out, out], [own, (2, s.cy, LANES), (2, s.cy, LANES)], v0, v1, mine, got
        )
    )


def solution(mesh):
    return jax.shard_map(
        shards,
        mesh=mesh,
        in_specs=(P("gz", "gy", None), P("gz", "gy", None)),
        out_specs=(P(None, "gz", "gy", None), P(None, "gz", "gy", None)),
        check_vma=False,
    )
```

```python
import functools

import jax
import jax.numpy as jnp
import numpy as np
from jax import lax
from jax.experimental import pallas as pl
from jax.experimental.pallas import tpu as pltpu
from jax.sharding import PartitionSpec as P


SPACING = 8
DAMPING = 8.0
LANES = 128
REACH = 3
F32 = jnp.float32
BF16 = jnp.bfloat16
VMEM = pl.BlockSpec(memory_space=pltpu.VMEM)
HBM = pl.BlockSpec(memory_space=pltpu.MemorySpace.HBM)
PARAMS = pltpu.CompilerParams(vmem_limit_bytes=20 * 1024 * 1024)


def round_up(value, step):
    return -(-value // step) * step


class Sizes:
    def __init__(self, shape):
        self.sz, self.sy, self.nx = shape
        self.cz, self.cy, self.cx = (n // SPACING for n in shape)
        self.na, self.nb = self.cz + 3, self.cy + 3
        self.bp = round_up(self.nb, 16)
        self.per = round_up(self.na * self.cx, LANES)
        self.wide = 3 * self.per
        self.tap = 4 * self.cx
        self.face = round_up(REACH * self.cx, LANES)
        self.used = REACH * self.cx
        self.own = self.cz * self.cx
        self.cells = 3 * self.cz * self.sy
        self.pair = 2 * self.cx
        assert 2 * 3 * self.pair == 3 * LANES and self.own == LANES
        self.block = self.cy + self.cy // 2 + 1
        assert self.tap % LANES == 0 and self.own % LANES == 0
        assert self.cy % 8 == 0 and self.bp == self.cy + 8 and self.cz > 1


def taps():
    t = (np.arange(SPACING) + 0.5) / SPACING
    return np.stack(
        [
            (1 - t) ** 3 / 6,
            (3 * t**3 - 6 * t**2 + 4) / 6,
            (-3 * t**3 + 3 * t**2 + 3 * t + 1) / 6,
            t**3 / 6,
        ]
    )


def basis(count, columns, offset):
    w = taps()
    out = np.zeros((count, columns))
    for v in range(count):
        for k in range(4):
            col = v // SPACING - 1 + k + offset
            if 0 <= col < columns:
                out[v, col] += w[k, v % SPACING]
    return out


def halves(matrix):
    high = np.asarray(matrix, np.float32).astype(jnp.bfloat16)
    low = (matrix - high.astype(np.float64)).astype(np.float32).astype(jnp.bfloat16)
    return high, low


def consts(s):
    by = basis(s.sy, s.bp, 1)
    yh, yl = halves(by)
    y_decode = np.concatenate([yh, yh, yl], 1)
    y_encode = np.concatenate([yh.T, yh.T, yl.T], 1)
    bx = basis(s.nx, s.cx, 0)
    w = taps()
    decode, encode = [], []
    for k in range(SPACING):
        high, low = halves(np.concatenate([w[t, k] * bx.T for t in range(4)], 0))
        encode.append(np.concatenate([high.T, low.T], 1))
    for sign in (1.0, -1.0):
        for k in range(SPACING // 2):
            parts = [0.5 * (w[t, k] + sign * w[3 - t, k]) * bx.T for t in range(2)]
            (h0, l0), (h1, l1) = (halves(v) for v in parts)
            flip = np.asarray(sign, jnp.bfloat16)
            zero = np.zeros((2 * s.cx, s.nx), jnp.bfloat16)
            decode.append(np.concatenate([h0, h1, flip * l1, flip * l0, h0, h1, zero], 0))
    return tuple(jnp.asarray(v) for v in (y_decode, np.stack(decode), y_encode, np.stack(encode)))


def gradient_consts(s):
    coef = {-3: -1.0, -2: 9.0, -1: -45.0, 1: 45.0, 2: -9.0, 3: 1.0}
    dx = np.zeros((s.nx, s.nx))
    for x in range(s.nx):
        for d, value in coef.items():
            if 0 <= x + d < s.nx:
                dx[x + d, x] = value
    dy = np.zeros((s.sy, s.sy + 16))
    for y in range(s.sy):
        for d, value in coef.items():
            at = y + d
            if at < 0:
                dy[y, s.sy + REACH + at] = value
            elif at >= s.sy:
                dy[y, s.sy + REACH + at - s.sy] = value
            else:
                dy[y, at] = value
    dx, dy = (v.astype(jnp.bfloat16) for v in (dx, dy))
    return jnp.asarray(np.concatenate([dx, dx], 0)), jnp.asarray(np.concatenate([dy, dy], 1))


def split(value):
    high = value.astype(BF16)
    return high, (value - high.astype(F32)).astype(BF16)


def dot(a, b):
    return jnp.dot(a, b, preferred_element_type=F32)


def rounded(value):
    return (value * F32(1.0 / 120.0)).astype(BF16).astype(F32)


def place(axis):
    index = lax.axis_index(axis)
    count = lax.axis_size(axis)
    return index > 0, index < count - 1, lax.rem(index, 2) == 0


def from_sides(even, a, b):
    return jnp.where(even, a, b), jnp.where(even, b, a)


def difference(near):
    return (
        45.0 * (near(1) - near(-1)) - 9.0 * (near(2) - near(-2)) + (near(3) - near(-3))
    )


def iota(shape, dim):
    return lax.broadcasted_iota(jnp.int32, shape, dim)


def roll(value, shift):
    shift = shift % value.shape[1]
    return pltpu.roll(value, shift, 1) if shift else value


def start_all(copies):
    for copy in copies:
        copy.start()
    return copies


def faces_z_kernel(s, f_ref, m_ref, za_ref, zb_ref, t_ref, sems):
    copies = []
    for i, ref in enumerate((f_ref, m_ref)):
        for j in range(2):
            z = pl.ds(j * (s.sz - REACH), REACH)
            copies.append(pltpu.make_async_copy(ref.at[z], t_ref.at[i, j], sems.at[i, j]))
    for copy in start_all(copies):
        copy.wait()
    even = place("gz")[2]
    down, up = (t_ref[0, j] + t_ref[1, j] for j in range(2))
    za_ref[...] = jnp.where(even, up, down)
    zb_ref[...] = jnp.where(even, down, up)


def faces_y_kernel(s, f_ref, m_ref, ya_ref, yb_ref):
    even = place("gy")[2]
    for k in range(REACH):
        high = s.sy - REACH + k
        down = f_ref[:, k, :] + m_ref[:, k, :]
        up = f_ref[:, high, :] + m_ref[:, high, :]
        ya_ref[k] = jnp.where(even, up, down)
        yb_ref[k] = jnp.where(even, down, up)


GROUP = 4


def start_kernel(s, f_ref, m_ref, dx_ref, sum_ref, diff_ref, gx_ref, gz_ref):
    dx = dx_ref[...]
    for i in range(s.sz // GROUP):
        planes = slice(i * GROUP, (i + 1) * GROUP)
        f, m = f_ref[planes], m_ref[planes]
        total = f + m
        sum_ref[planes] = total
        diff_ref[planes] = f - m
        sh, sl = split(total.reshape(GROUP * s.sy, s.nx))
        gx = rounded(dot(jnp.concatenate([sh, sl], 1), dx))
        gx_ref[planes] = gx.reshape(GROUP, s.sy, s.nx)

    def step(i, carry):
        for y in range(0, s.sy, 16):
            rows = slice(y, y + 16)
            gz_ref[i, rows] = rounded(difference(lambda d: sum_ref[i + REACH + d, rows]))
        return carry

    lax.fori_loop(0, s.sz - 2 * REACH, step, 0)


def edge_planes(s):
    return [z < REACH or z >= s.sz - REACH for z in range(s.sz)]


def put_volume(s, row, z, rows, diff_ref, grads, high_ref, low_ref):
    mm = diff_ref[z, rows]
    for c in range(3):
        high, low = split(mm * grads[c])
        at = slice(row + c * s.sy + rows.start, row + c * s.sy + rows.stop)
        high_ref[at, :] = high
        low_ref[at, :] = low


def inner_kernel(
    s, sum_ref, diff_ref, gx_ref, gz_ref, ra_ref, rb_ref, dy_ref, re_ref,
    gy_ref, acc_ref, h_ref, vh0, vh1, vl0, vl1,
):
    below, above, even = place("gy")
    h_ref[...] = jnp.zeros_like(h_ref)
    for k in range(REACH):
        up, down = from_sides(even, ra_ref[k], rb_ref[k])
        h_ref[:, k, :] = jnp.where(below, down, 0.0)
        h_ref[:, REACH + k, :] = jnp.where(above, up, 0.0)
    dy = dy_ref[...]

    def step(i, carry):
        for j in range(GROUP):
            z = i * GROUP + j
            sh, sl = split(sum_ref[z])
            hh, hl = split(h_ref[z])
            gy_ref[z] = rounded(dot(dy, jnp.concatenate([sh, hh, sl, hl], 0)))
        return carry

    lax.fori_loop(0, s.sz // GROUP, step, 0)
    waits = edge_planes(s)
    part = 3 * s.sy
    acc_ref[...] = jnp.zeros_like(acc_ref)
    for k in range(SPACING):
        vh, vl = ((vh0, vl0), (vh1, vl1))[k % 2]
        ready = [zc for zc in range(s.cz) if not waits[zc * SPACING + k]]
        for zc in ready:
            z = zc * SPACING + k
            for y in range(0, s.sy, 16):
                rows = slice(y, y + 16)
                grads = [r[i, rows] for r, i in ((gz_ref, z - REACH), (gy_ref, z), (gx_ref, z))]
                put_volume(s, zc * part, z, rows, diff_ref, grads, vh, vl)
        at = slice(ready[0] * part, (ready[-1] + 1) * part)
        weights = re_ref[k]
        acc_ref[at, :] += dot(
            jnp.concatenate([vh[at, :], vl[at, :]], 1), jnp.concatenate([weights, weights], 0)
        )


def edge_kernel(
    s, sum_ref, diff_ref, gx_ref, gy_ref, ra_ref, rb_ref, acc_in, ye_ref, re_ref,
    gz_ref, p_ref, za_ref, zb_ref, h_ref, vh_ref, vl_ref, acc_ref,
):
    below, above, even = place("gz")
    for k in range(REACH):
        up, down = from_sides(even, ra_ref[k], rb_ref[k])
        h_ref[k] = jnp.where(below, down, 0.0)
        h_ref[REACH + k] = jnp.where(above, up, 0.0)
    part = 3 * s.sy
    for side, zc in ((0, 0), (1, s.cz - 1)):
        first = 0 if side == 0 else s.sz - REACH
        for j in range(REACH):
            z = first + j
            for y in range(0, s.sy, 16):
                rows = slice(y, y + 16)

                def near(d):
                    if z + d < 0:
                        return h_ref[z + d + REACH, rows]
                    if z + d >= s.sz:
                        return h_ref[REACH + z + d - s.sz, rows]
                    return sum_ref[z + d, rows]

                gz = rounded(difference(near))
                gz_ref[side * REACH + j, rows] = gz
                row = (side * REACH + j) * part
                grads = [gz, gy_ref[z, rows], gx_ref[z, rows]]
                put_volume(s, row, z, rows, diff_ref, grads, vh_ref, vl_ref)
        lhs, rhs = [], []
        for j in range(REACH):
            row = (side * REACH + j) * part
            weights = re_ref[(first + j) % SPACING]
            for ref in (vh_ref, vl_ref):
                lhs.append(ref[row : row + part, :])
                rhs.append(weights)
        at = slice(zc * part, (zc + 1) * part)
        acc_ref[at, :] = acc_in[at, :] + dot(jnp.concatenate(lhs, 1), jnp.concatenate(rhs, 0))
    encode_y(s, [acc_ref] + [acc_in] * (s.cz - 2) + [acc_ref], ye_ref, p_ref)
    send_faces(s, p_ref, za_ref, zb_ref)


def encode_y(s, acc_refs, ye_ref, p_ref):
    columns = []
    for i in range(3 * s.cz):
        both = acc_refs[i // 3][i * s.sy : (i + 1) * s.sy, :]
        columns.append(both[:, : s.tap] + both[:, s.tap :])
    high, low = split(jnp.concatenate(columns, 1))
    out = dot(ye_ref[...], jnp.concatenate([high, low, high], 0))
    for c in range(3):
        total = jnp.zeros((s.bp, s.per), F32)
        for zc in range(s.cz):
            at = (zc * 3 + c) * s.tap
            cell = out[:, at : at + s.tap]
            if s.per > s.tap:
                cell = jnp.concatenate([cell, jnp.zeros((s.bp, s.per - s.tap), F32)], 1)
            total = total + roll(cell, zc * s.cx)
        p_ref[:, c * s.per : (c + 1) * s.per] = total


def send_faces(s, p_ref, za_ref, zb_ref):
    even = place("gz")[2]
    for c in range(3):
        low = c * s.per
        down = p_ref[:, low : low + s.face]
        up = p_ref[:, low + s.own : low + s.own + s.face]
        at = slice(c * s.face, (c + 1) * s.face)
        to_a, to_b = jnp.where(even, up, down), jnp.where(even, down, up)
        for i in range(za_ref.shape[0]):
            za_ref[i, :, at] = to_a[4 * i : 4 * i + 4]
            zb_ref[i, :, at] = to_b[4 * i : 4 * i + 4]


def fold_z_kernel(s, p_ref, ra_ref, rb_ref, o_ref, ya_ref, yb_ref):
    below, above, even = place("gz")
    layer = iota((s.bp, s.per), 1) // s.cx
    first = jnp.where(below, 0, 1)
    last = jnp.where(above, s.cz + 2, s.cz)
    inside = (layer >= first) & (layer <= last)
    shared = iota((4, s.face), 1) < s.used
    for c in range(3):
        low = c * s.per
        high = low + s.own
        at = slice(c * s.face, (c + 1) * s.face)
        o_ref[:, low : low + s.per] = jnp.where(inside, p_ref[:, low : low + s.per], 0.0)
        for i in range(ra_ref.shape[0]):
            rows = slice(4 * i, 4 * i + 4)
            up, down = from_sides(even, ra_ref[i, :, at], rb_ref[i, :, at])
            o_ref[rows, low : low + s.face] += jnp.where(shared & below, down, 0.0)
            o_ref[rows, high : high + s.face] += jnp.where(shared & above, up, 0.0)
    even = place("gy")[2]
    down, up = o_ref[:4, :], o_ref[s.cy : s.cy + 4, :]
    ya_ref[...] = jnp.where(even, up, down)
    yb_ref[...] = jnp.where(even, down, up)


def fold_y(s, p_ref, ra_ref, rb_ref, v_ref):
    below, above, even = place("gy")
    up, down = from_sides(even, ra_ref[...], rb_ref[...])
    row = iota((s.bp, s.wide), 0)
    inside = (row >= jnp.where(below, 0, 1)) & (row <= jnp.where(above, s.cy + 2, s.cy))
    v_ref[...] = jnp.where(inside, p_ref[...], 0.0)
    shared = iota((4, s.wide), 0) < REACH
    v_ref[:4, :] += jnp.where(shared & below, down, 0.0)
    v_ref[s.cy : s.cy + 4, :] += jnp.where(shared & above, up, 0.0)


def own_part(s, v_ref, out_ref):
    for c in range(3):
        rows = v_ref[1 : s.cy + 1, c * s.per : (c + 1) * s.per]
        out_ref[:, c * s.own : (c + 1) * s.own] = roll(rows, -s.cx)[:, : s.own]


def operate(s, v_ref, yd_ref, rd_ref, re_ref, grads, scratch):
    even_ref, odd_ref, *pairs, acc_ref = scratch
    cells = []
    for zc in range(s.cz):
        for c in range(3):
            lanes = v_ref[:, c * s.per : (c + 1) * s.per]
            cell = roll(lanes, -zc * s.cx)[:, : s.tap]
            group = iota(cell.shape, 1) // s.cx % 2
            back = jnp.where(group == 0, roll(cell, s.cx), roll(cell, 3 * s.cx))
            cells += [cell + back, cell - back]
    ph, plow = split(jnp.concatenate(cells, 1))
    inner = dot(yd_ref[...], jnp.concatenate([ph, plow, ph], 0))
    for i in range(3 * s.cz):
        at = slice(i * s.sy, (i + 1) * s.sy)
        for j, ref in enumerate((even_ref, odd_ref)):
            low = (2 * i + j) * s.tap
            ref[at, :] = jnp.concatenate(split(inner[:, low : low + s.tap]), 1)
    gz_inner, gz_edge, gy_ref, gx_ref = grads
    square = jnp.zeros((16, s.nx), F32)
    half = SPACING // 2
    for k in range(half):
        fe_ref, fo_ref, w0, w1 = pairs[4 * (k % 2) : 4 * (k % 2) + 4]
        fe_ref[...] = dot(even_ref[...], rd_ref[k])
        fo_ref[...] = dot(odd_ref[...], rd_ref[half + k])
        for zc in range(s.cz):
            for y in range(0, s.sy, 16):
                rows = slice(y, y + 16)
                at = [
                    slice((zc * 3 + c) * s.sy + y, (zc * 3 + c) * s.sy + y + 16) for c in range(3)
                ]
                even = [fe_ref[i, :] for i in at]
                odd = [fo_ref[i, :] for i in at]
                for sign, v, w_ref in ((1, k, w0), (-1, SPACING - 1 - k, w1)):
                    z = zc * SPACING + v
                    if z < REACH:
                        gz_ref, iz = gz_edge, z
                    elif z >= s.sz - REACH:
                        gz_ref, iz = gz_edge, REACH + z - (s.sz - REACH)
                    else:
                        gz_ref, iz = gz_inner, z - REACH
                    g = [r[i, rows] for r, i in ((gz_ref, iz), (gy_ref, z), (gx_ref, z))]
                    f = [e + o if sign > 0 else e - o for e, o in zip(even, odd)]
                    dotted = g[0] * f[0] + g[1] * f[1] + g[2] * f[2]
                    square = square + dotted * dotted
                    for c in range(3):
                        w_ref[at[c], :] = (g[c] * dotted).astype(BF16)
        add = dot(
            jnp.concatenate([w0[...], w1[...]], 1),
            jnp.concatenate([re_ref[k], re_ref[SPACING - 1 - k]], 0),
        )
        acc_ref[...] = add if k == 0 else acc_ref[...] + add
    return square


def total_of(value):
    return jnp.sum(value, keepdims=True)


def moments(sums, start):
    lane = iota((1, LANES), 1)
    out = jnp.zeros((1, LANES), F32)
    for k, value in enumerate(sums):
        out = jnp.where(lane == start + k, value, out)
    return out


def apply_kernel(
    s, p_ref, ra_ref, rb_ref, gi_ref, ge_ref, gy_ref, gx_ref, yd_ref, rd_ref, ye_ref, re_ref,
    o_ref, za_ref, zb_ref, own_ref, sum_ref, v_ref, *scratch,
):
    fold_y(s, p_ref, ra_ref, rb_ref, v_ref)
    own_part(s, v_ref, own_ref)
    square = operate(
        s, v_ref, yd_ref, rd_ref, re_ref, (gi_ref, ge_ref, gy_ref, gx_ref), scratch
    )
    encode_y(s, [scratch[-1]] * s.cz, ye_ref, o_ref)
    send_faces(s, o_ref, za_ref, zb_ref)
    own = own_ref[...]
    sum_ref[...] = moments([total_of(own * own), total_of(square)], 0)


NEIGHBOURS = [(dz, dy) for dz in (-1, 0, 1) for dy in (-1, 0, 1) if dz or dy]


def neighbour(dz, dy):
    nz, ny = lax.axis_size("gz"), lax.axis_size("gy")
    iz, iy = lax.axis_index("gz"), lax.axis_index("gy")
    tz, ty = iz + dz, iy + dy
    ok = (tz >= 0) & (tz < nz) & (ty >= 0) & (ty < ny)
    return ok, jnp.where(ok, tz * ny + ty, iz * ny + iy)


def last_kernel(
    s, p_ref, ra_ref, rb_ref, gi_ref, ge_ref, gy_ref, gx_ref, m_ref,
    yd_ref, rd_ref, ye_ref, re_ref,
    own_ref, part_ref, send_ref, v_ref, o_ref, t_ref, y_ref, *scratch,
):
    fold_y(s, p_ref, ra_ref, rb_ref, v_ref)
    own_part(s, v_ref, own_ref)
    square = operate(
        s, v_ref, yd_ref, rd_ref, re_ref, (gi_ref, ge_ref, gy_ref, gx_ref), scratch
    )
    own = own_ref[...]
    sums = m_ref[...] + moments([total_of(own * own), total_of(square)], 2)
    encode_y(s, [scratch[-1]] * s.cz, ye_ref, o_ref)
    own_part(s, o_ref, part_ref)
    for d in range(send_ref.shape[0]):
        send_ref[d, s.block - 1, :, :] = sums
    lane = iota((s.bp, 2 * LANES), 1)
    t_ref[...] = jnp.zeros_like(t_ref)
    for i, dz in enumerate((-1, 1)):
        layer = 0 if dz < 0 else s.cz + 1
        width = s.cx if dz < 0 else s.pair
        total = jnp.zeros((s.bp, 2 * LANES), F32)
        for c in range(3):
            low = c * s.pair
            lanes = roll(o_ref[:, c * s.per : (c + 1) * s.per], low - layer * s.cx)
            total = jnp.where((lane >= low) & (lane < low + width), lanes[:, : 2 * LANES], total)
        t_ref[i, 8 : 8 + s.bp, :] = total
    for c in range(3):
        lanes = roll(o_ref[:, c * s.per : (c + 1) * s.per], -s.cx)
        y_ref[:, c * s.own : (c + 1) * s.own] = lanes[:, : s.own]
    half = s.cy // 2
    low_half = iota((half, LANES), 1) < LANES // 2
    for dz, dy in NEIGHBOURS:
        _, target = neighbour(dz, dy)
        if dz:
            start = 9 + dy * s.cy
            side = (dz + 1) // 2
            send_ref[target, 0 : s.cy, 0, :] = t_ref[side, start : start + s.cy, :LANES]
            near = t_ref[side, start : start + half, LANES:]
            far = t_ref[side, start + half : start + s.cy, LANES:]
            send_ref[target, s.cy : s.cy + half, 0, :] = jnp.where(
                low_half, near, roll(far, LANES // 2)
            )
        else:
            for c in range(3):
                lanes = slice(c * s.own, (c + 1) * s.own)
                if dy > 0:
                    send_ref[target, 2 * c : 2 * c + 2, 0, :] = y_ref[s.cy + 1 : s.cy + 3, lanes]
                else:
                    send_ref[target, c, :, :] = y_ref[0:1, lanes]


def finish_kernel(s, v0_ref, v1_ref, part_ref, got_ref, u_ref, r_ref, v_ref, t_ref, w_ref):
    v_ref[...] = part_ref[...]
    half = s.cy // 2
    for i, dz in enumerate((-1, 1)):
        first = jnp.zeros((s.cy, LANES), F32)
        rest = jnp.zeros((half, LANES), F32)
        for dy in (-1, 0, 1):
            ok, source = neighbour(dz, dy)
            first += jnp.where(ok, got_ref[source, 0 : s.cy, 0, :], 0.0)
            rest += jnp.where(ok, got_ref[source, s.cy : s.cy + half, 0, :], 0.0)
        t_ref[i] = first
        w_ref[i, 0:half, :] = rest
        w_ref[i, half:, :] = roll(rest, LANES // 2)

    lane = iota((s.cy, s.own), 1)
    for c in range(3):
        lanes = slice(c * s.own, (c + 1) * s.own)
        first, last = (w_ref[0], w_ref[1]) if c == 2 else (t_ref[0], t_ref[1])
        low = c % 2 * s.pair
        v_ref[:, lanes] += jnp.where(lane < s.pair, roll(first, -low), 0.0)
        last = roll(last, (s.cz - 1) * s.cx - low)
        v_ref[:, lanes] += jnp.where(lane >= s.own - s.cx, last, 0.0)
    for dy in (-1, 1):
        ok, source = neighbour(0, dy)
        for c in range(3):
            lanes = slice(c * s.own, (c + 1) * s.own)
            if dy < 0:
                value = got_ref[source, 2 * c : 2 * c + 2, 0, :]
                v_ref[0:2, lanes] += jnp.where(ok, value, 0.0)
            else:
                v_ref[s.cy - 1 : s.cy, lanes] += jnp.where(ok, got_ref[source, c, :, :], 0.0)

    tot = jnp.sum(got_ref[:, s.block - 1, 0, :], axis=0, keepdims=True)
    m0, m1, m2, m3 = (tot[:, k : k + 1] for k in range(4))
    v0, v1, v2 = v0_ref[...], v1_ref[...], v_ref[...]
    rho = m1 / m0
    a0 = 1.0 / (rho + DAMPING)
    rr1 = a0 * a0 * (m2 - rho * m1)
    beta = rr1 / m0
    quad = a0 * a0 * (m3 - 2.0 * rho * m2 + rho * rho * m1) + DAMPING * rr1
    a1 = rr1 / (quad - beta * rr1 / a0)
    r1 = a0 * (rho * v0 - v1)
    image = a0 * (rho * v1 - v2) + DAMPING * r1 + beta * (v1 + DAMPING * v0)
    update = a0 * v0 + a1 * (r1 + beta * v0)
    residual = r1 - a1 * image
    for out_ref, value in ((u_ref, update), (r_ref, residual)):
        for c in range(3):
            for a in range(s.cz):
                at = c * s.own + a * s.cx
                out_ref[c, a] = value[:, at : at + s.cx]


def swap(value_a, value_b, axis):
    count = lax.axis_size(axis)
    even = [(i, i ^ 1) for i in range(count)]
    odd = [(i, (i + (1 if i % 2 else -1)) % count) for i in range(count)]
    value_b = lax.ppermute(value_b, axis, odd)
    return lax.ppermute(value_a, axis, even), value_b


def scratch_of(item):
    if not isinstance(item, tuple):
        return item
    return pltpu.VMEM(*(item if isinstance(item[0], tuple) else (item, F32)))


def call(kernel, outs, scratch, *args, far=0):
    shapes = [jax.ShapeDtypeStruct(o, F32) for o in outs]
    return pl.pallas_call(
        kernel,
        out_shape=shapes,
        in_specs=[HBM] * far + [VMEM] * (len(args) - far),
        out_specs=[VMEM] * len(outs),
        scratch_shapes=[scratch_of(n) for n in scratch],
        compiler_params=PARAMS,
    )(*[pltpu.with_memory_space_constraint(v, pltpu.HBM) for v in args[:far]], *args[far:])


def shards(fixed, moving):
    s = Sizes(fixed.shape)
    devices = lax.axis_size("gz") * lax.axis_size("gy")
    dx, dy = gradient_consts(s)
    yd, rd, ye, re = consts(s)
    part = functools.partial

    zhalo, yhalo = (REACH, s.sy, s.nx), (REACH, s.sz, s.nx)
    za, zb = call(
        part(faces_z_kernel, s),
        [zhalo, zhalo],
        [(2, 2, *zhalo), pltpu.SemaphoreType.DMA((2, 2))],
        fixed, moving, far=2,
    )
    za, zb = swap(za, zb, "gz")
    ya, yb = call(part(faces_y_kernel, s), [yhalo, yhalo], [], fixed, moving)
    ya, yb = swap(ya, yb, "gy")
    volume = fixed.shape
    total, diff, gx, gz_inner = call(
        part(start_kernel, s),
        [volume, volume, volume, (s.sz - 2 * REACH, s.sy, s.nx)],
        [],
        fixed, moving, dx,
    )
    acc = (s.cells, 2 * s.tap)
    half = ((s.cells, s.nx), BF16)
    gy, inner = call(
        part(inner_kernel, s),
        [volume, acc],
        [(s.sz, 16, s.nx), half, half, half, half],
        total, diff, gx, gz_inner, ya, yb, dy, re,
    )
    grid, zface, yface = (s.bp, s.wide), (round_up(s.nb, 4) // 4, 4, 3 * s.face), (4, s.wide)
    few = ((2 * REACH * 3 * s.sy, s.nx), BF16)
    gz_edge, grid0, za, zb = call(
        part(edge_kernel, s),
        [(2 * REACH, s.sy, s.nx), grid, zface, zface],
        [(2 * REACH, s.sy, s.nx), few, few, acc],
        total, diff, gx, gy, za, zb, inner, ye, re,
    )

    def fold_z(value, za, zb):
        za, zb = swap(za, zb, "gz")
        value, ya, yb = call(part(fold_z_kernel, s), [grid, yface, yface], [], value, za, zb)
        return (value, *swap(ya, yb, "gy"))

    own = (s.cy, 3 * s.own)
    field = (s.cells, s.nx)
    left = ((s.cells, 2 * s.tap), BF16)
    work = [left, left, *[field, field, half, half] * 2, acc]
    grads = (gz_inner, gz_edge, gy, gx)
    grid1, za, zb, v0, sums = call(
        part(apply_kernel, s),
        [grid, zface, zface, own, (1, LANES)],
        [grid, *work],
        *fold_z(grid0, za, zb), *grads, yd, rd, ye, re,
    )
    v1, mine, send = call(
        part(last_kernel, s),
        [own, own, (devices, s.block, 1, LANES)],
        [grid, grid, (2, 16 + s.bp, 2 * LANES), (s.bp, 3 * s.own), *work],
        *fold_z(grid1, za, zb), *grads, sums, yd, rd, ye, re,
    )
    got = lax.all_to_all(send, ("gz", "gy"), 0, 0)
    out = (3, s.cz, s.cy, s.cx)
    return tuple(
        call(
            part(finish_kernel, s), [out, out], [own, (2, s.cy, LANES), (2, s.cy, LANES)], v0, v1, mine, got
        )
    )


def solution(mesh):
    return jax.shard_map(
        shards,
        mesh=mesh,
        in_specs=(P("gz", "gy", None), P("gz", "gy", None)),
        out_specs=(P(None, "gz", "gy", None), P(None, "gz", "gy", None)),
        check_vma=False,
    )
```

```python
import functools

import jax
import jax.numpy as jnp
import numpy as np
from jax import lax
from jax.experimental import pallas as pl
from jax.experimental.pallas import tpu as pltpu
from jax.sharding import PartitionSpec as P


SPACING = 8
DAMPING = 8.0
LANES = 128
REACH = 3
F32 = jnp.float32
BF16 = jnp.bfloat16
VMEM = pl.BlockSpec(memory_space=pltpu.VMEM)
HBM = pl.BlockSpec(memory_space=pltpu.MemorySpace.HBM)
PARAMS = pltpu.CompilerParams(vmem_limit_bytes=20 * 1024 * 1024)


def round_up(value, step):
    return -(-value // step) * step


class Sizes:
    def __init__(self, shape):
        self.sz, self.sy, self.nx = shape
        self.cz, self.cy, self.cx = (n // SPACING for n in shape)
        self.na, self.nb = self.cz + 3, self.cy + 3
        self.bp = round_up(self.nb, 16)
        self.per = round_up(self.na * self.cx, LANES)
        self.wide = 3 * self.per
        self.tap = 4 * self.cx
        self.face = round_up(REACH * self.cx, LANES)
        self.used = REACH * self.cx
        self.own = self.cz * self.cx
        self.cells = 3 * self.cz * self.sy
        self.pair = 2 * self.cx
        assert 2 * 3 * self.pair == 3 * LANES and self.own == LANES
        self.block = self.cy + self.cy // 2 + 1
        assert self.tap % LANES == 0 and self.own % LANES == 0
        assert self.cy % 8 == 0 and self.bp == self.cy + 8 and self.cz > 1
        assert self.sy % 16 == 0 and self.sy > 32


def taps():
    t = (np.arange(SPACING) + 0.5) / SPACING
    return np.stack(
        [
            (1 - t) ** 3 / 6,
            (3 * t**3 - 6 * t**2 + 4) / 6,
            (-3 * t**3 + 3 * t**2 + 3 * t + 1) / 6,
            t**3 / 6,
        ]
    )


def basis(count, columns, offset):
    w = taps()
    out = np.zeros((count, columns))
    for v in range(count):
        for k in range(4):
            col = v // SPACING - 1 + k + offset
            if 0 <= col < columns:
                out[v, col] += w[k, v % SPACING]
    return out


def halves(matrix):
    high = np.asarray(matrix, np.float32).astype(jnp.bfloat16)
    low = (matrix - high.astype(np.float64)).astype(np.float32).astype(jnp.bfloat16)
    return high, low


def consts(s):
    by = basis(s.sy, s.bp, 1)
    yh, yl = halves(by)
    y_decode = np.concatenate([yh, yh, yl], 1)
    y_encode = np.concatenate([yh.T, yh.T, yl.T], 1)
    bx = basis(s.nx, s.cx, 0)
    w = taps()
    decode, encode = [], []
    for k in range(SPACING):
        high, low = halves(np.concatenate([w[t, k] * bx.T for t in range(4)], 0))
        encode.append(np.concatenate([high.T, low.T], 1))
    for sign in (1.0, -1.0):
        for k in range(SPACING // 2):
            parts = [0.5 * (w[t, k] + sign * w[3 - t, k]) * bx.T for t in range(2)]
            (h0, l0), (h1, l1) = (halves(v) for v in parts)
            flip = np.asarray(sign, jnp.bfloat16)
            zero = np.zeros((2 * s.cx, s.nx), jnp.bfloat16)
            decode.append(np.concatenate([h0, h1, flip * l1, flip * l0, h0, h1, zero], 0))
    return tuple(jnp.asarray(v) for v in (y_decode, np.stack(decode), y_encode, np.stack(encode)))


def gradient_consts(s):
    coef = {-3: -1.0, -2: 9.0, -1: -45.0, 1: 45.0, 2: -9.0, 3: 1.0}
    dx = np.zeros((s.nx, s.nx))
    for x in range(s.nx):
        for d, value in coef.items():
            if 0 <= x + d < s.nx:
                dx[x + d, x] = value
    dy = np.zeros((s.sy, s.sy + 16))
    for y in range(s.sy):
        for d, value in coef.items():
            at = y + d
            if at < 0:
                dy[y, s.sy + REACH + at] = value
            elif at >= s.sy:
                dy[y, s.sy + REACH + at - s.sy] = value
            else:
                dy[y, at] = value
    own, halo = dy[:, : s.sy], dy[:, s.sy :]
    halo = np.concatenate([halo[:8], halo[-8:]], 0)
    pairs = (np.concatenate([dx, dx], 0), *(np.concatenate([v, v], 1) for v in (own, halo)))
    return tuple(jnp.asarray(v.astype(jnp.bfloat16)) for v in pairs)


def split(value):
    high = value.astype(BF16)
    return high, (value - high.astype(F32)).astype(BF16)


def dot(a, b):
    return jnp.dot(a, b, preferred_element_type=F32)


def rounded(value):
    return (value * F32(1.0 / 120.0)).astype(BF16).astype(F32)


def place(axis):
    index = lax.axis_index(axis)
    count = lax.axis_size(axis)
    return index > 0, index < count - 1, lax.rem(index, 2) == 0


def from_sides(even, a, b):
    return jnp.where(even, a, b), jnp.where(even, b, a)


def difference(near):
    return (
        45.0 * (near(1) - near(-1)) - 9.0 * (near(2) - near(-2)) + (near(3) - near(-3))
    )


def iota(shape, dim):
    return lax.broadcasted_iota(jnp.int32, shape, dim)


def roll(value, shift):
    shift = shift % value.shape[1]
    return pltpu.roll(value, shift, 1) if shift else value


def start_all(copies):
    for copy in copies:
        copy.start()
    return copies


def faces_z_kernel(s, f_ref, m_ref, za_ref, zb_ref, t_ref, sems):
    copies = []
    for i, ref in enumerate((f_ref, m_ref)):
        for j in range(2):
            z = pl.ds(j * (s.sz - REACH), REACH)
            copies.append(pltpu.make_async_copy(ref.at[z], t_ref.at[i, j], sems.at[i, j]))
    for copy in start_all(copies):
        copy.wait()
    even = place("gz")[2]
    down, up = (t_ref[0, j] + t_ref[1, j] for j in range(2))
    za_ref[...] = jnp.where(even, up, down)
    zb_ref[...] = jnp.where(even, down, up)


def faces_y_kernel(s, f_ref, m_ref, ya_ref, yb_ref):
    even = place("gy")[2]
    for k in range(REACH):
        high = s.sy - REACH + k
        down = f_ref[:, k, :] + m_ref[:, k, :]
        up = f_ref[:, high, :] + m_ref[:, high, :]
        ya_ref[k] = jnp.where(even, up, down)
        yb_ref[k] = jnp.where(even, down, up)


GROUP = 4


def start_kernel(s, f_ref, m_ref, dx_ref, sum_ref, diff_ref, gx_ref, gz_ref):
    dx = dx_ref[...]
    for i in range(s.sz // GROUP):
        planes = slice(i * GROUP, (i + 1) * GROUP)
        f, m = f_ref[planes], m_ref[planes]
        total = f + m
        sum_ref[planes] = total
        diff_ref[planes] = f - m
        sh, sl = split(total.reshape(GROUP * s.sy, s.nx))
        gx = rounded(dot(jnp.concatenate([sh, sl], 1), dx))
        gx_ref[planes] = gx.reshape(GROUP, s.sy, s.nx)

    def step(i, carry):
        for y in range(0, s.sy, 16):
            rows = slice(y, y + 16)
            gz_ref[i, rows] = rounded(difference(lambda d: sum_ref[i + REACH + d, rows]))
        return carry

    lax.fori_loop(0, s.sz - 2 * REACH, step, 0)


def edge_planes(s):
    return [z < REACH or z >= s.sz - REACH for z in range(s.sz)]


def put_volume(row_of, z, rows, diff_ref, grads, high_ref, low_ref):
    mm = diff_ref[z, rows]
    for c in range(3):
        high, low = split(mm * grads[c])
        at = slice(row_of(c), row_of(c) + rows.stop - rows.start)
        high_ref[at, :] = high
        low_ref[at, :] = low


def gy_rows(s, gy_ref, side_ref, z, rows):
    if rows.start == 0:
        return jnp.concatenate([side_ref[z, :8], gy_ref[z, 8:16]], 0)
    if rows.stop == s.sy:
        return jnp.concatenate([gy_ref[z, s.sy - 16 : s.sy - 8], side_ref[z, 8:]], 0)
    return gy_ref[z, rows]


def encode_planes(s, starts, diff_ref, gx_ref, gz_ref, gy_of, re_ref, acc_ref, scratch):
    waits = edge_planes(s)
    count = 16 * len(starts)
    part = 3 * count
    acc_ref[...] = jnp.zeros_like(acc_ref)
    for k in range(SPACING):
        vh, vl = scratch[2 * (k % 2) : 2 * (k % 2) + 2]
        ready = [zc for zc in range(s.cz) if not waits[zc * SPACING + k]]
        for zc in ready:
            z = zc * SPACING + k
            for i, y in enumerate(starts):
                rows = slice(y, y + 16)
                grads = [gz_ref[z - REACH, rows], gy_of(z, rows), gx_ref[z, rows]]
                base = zc * part + 16 * i
                put_volume(lambda c: base + c * count, z, rows, diff_ref, grads, vh, vl)
        at = slice(ready[0] * part, (ready[-1] + 1) * part)
        weights = re_ref[k]
        acc_ref[at, :] += dot(
            jnp.concatenate([vh[at, :], vl[at, :]], 1), jnp.concatenate([weights, weights], 0)
        )


def inner_kernel(
    s, sum_ref, diff_ref, gx_ref, gz_ref, dy_ref, re_ref, gy_ref, raw_ref, acc_ref, *scratch
):
    dy = dy_ref[...]

    def step(i, carry):
        for j in range(GROUP):
            z = i * GROUP + j
            sh, sl = split(sum_ref[z])
            value = dot(dy, jnp.concatenate([sh, sl], 0))
            raw_ref[z] = jnp.concatenate([value[:8], value[s.sy - 8 :]], 0)
            gy_ref[z] = rounded(value)
        return carry

    lax.fori_loop(0, s.sz // GROUP, step, 0)
    starts = range(16, s.sy - 16, 16)
    encode_planes(
        s, starts, diff_ref, gx_ref, gz_ref, lambda z, rows: gy_ref[z, rows], re_ref, acc_ref, scratch
    )


def side_kernel(
    s, diff_ref, gx_ref, gz_ref, gy_ref, raw_ref, ra_ref, rb_ref, dy_ref, re_ref,
    side_ref, acc_ref, h_ref, *scratch,
):
    below, above, even = place("gy")
    h_ref[...] = jnp.zeros_like(h_ref)
    for k in range(REACH):
        up, down = from_sides(even, ra_ref[k], rb_ref[k])
        h_ref[:, k, :] = jnp.where(below, down, 0.0)
        h_ref[:, REACH + k, :] = jnp.where(above, up, 0.0)
    dy = dy_ref[...]

    def step(i, carry):
        for j in range(GROUP):
            z = i * GROUP + j
            add = dot(dy, jnp.concatenate(split(h_ref[z]), 0))
            side_ref[z] = rounded(raw_ref[z] + add)
        return carry

    lax.fori_loop(0, s.sz // GROUP, step, 0)
    encode_planes(
        s, (0, s.sy - 16), diff_ref, gx_ref, gz_ref,
        lambda z, rows: gy_rows(s, gy_ref, side_ref, z, rows), re_ref, acc_ref, scratch,
    )


def edge_kernel(
    s, sum_ref, diff_ref, gx_ref, gy_ref, gs_ref, ra_ref, rb_ref, mid_ref, side_ref, ye_ref, re_ref,
    gz_ref, p_ref, za_ref, zb_ref, h_ref, vh_ref, vl_ref, acc_ref,
):
    below, above, even = place("gz")
    for k in range(REACH):
        up, down = from_sides(even, ra_ref[k], rb_ref[k])
        h_ref[k] = jnp.where(below, down, 0.0)
        h_ref[REACH + k] = jnp.where(above, up, 0.0)
    part = 3 * s.sy
    for side in (0, 1):
        first = 0 if side == 0 else s.sz - REACH
        for j in range(REACH):
            z = first + j
            for y in range(0, s.sy, 16):
                rows = slice(y, y + 16)

                def near(d):
                    if z + d < 0:
                        return h_ref[z + d + REACH, rows]
                    if z + d >= s.sz:
                        return h_ref[REACH + z + d - s.sz, rows]
                    return sum_ref[z + d, rows]

                gz = rounded(difference(near))
                gz_ref[side * REACH + j, rows] = gz
                row = (side * REACH + j) * part + y
                grads = [gz, gy_rows(s, gy_ref, gs_ref, z, rows), gx_ref[z, rows]]
                put_volume(lambda c: row + c * s.sy, z, rows, diff_ref, grads, vh_ref, vl_ref)
        lhs, rhs = [], []
        for j in range(REACH):
            row = (side * REACH + j) * part
            weights = re_ref[(first + j) % SPACING]
            for ref in (vh_ref, vl_ref):
                lhs.append(ref[row : row + part, :])
                rhs.append(weights)
        at = slice(side * part, (side + 1) * part)
        acc_ref[at, :] = dot(jnp.concatenate(lhs, 1), jnp.concatenate(rhs, 0))

    def rows_of(i):
        inner = s.sy - 32
        both = jnp.concatenate(
            [
                side_ref[32 * i : 32 * i + 16, :],
                mid_ref[inner * i : inner * (i + 1), :],
                side_ref[32 * i + 16 : 32 * i + 32, :],
            ],
            0,
        )
        zc, c = divmod(i, 3)
        if zc in (0, s.cz - 1):
            row = (3 * (zc > 0) + c) * s.sy
            both = both + acc_ref[row : row + s.sy, :]
        return both

    encode_y(s, rows_of, ye_ref, p_ref)
    send_faces(s, p_ref, za_ref, zb_ref)


def encode_y(s, rows_of, ye_ref, p_ref):
    columns = []
    for i in range(3 * s.cz):
        both = rows_of(i)
        columns.append(both[:, : s.tap] + both[:, s.tap :])
    high, low = split(jnp.concatenate(columns, 1))
    out = dot(ye_ref[...], jnp.concatenate([high, low, high], 0))
    for c in range(3):
        total = jnp.zeros((s.bp, s.per), F32)
        for zc in range(s.cz):
            at = (zc * 3 + c) * s.tap
            cell = out[:, at : at + s.tap]
            if s.per > s.tap:
                cell = jnp.concatenate([cell, jnp.zeros((s.bp, s.per - s.tap), F32)], 1)
            total = total + roll(cell, zc * s.cx)
        p_ref[:, c * s.per : (c + 1) * s.per] = total


def send_faces(s, p_ref, za_ref, zb_ref):
    even = place("gz")[2]
    for c in range(3):
        low = c * s.per
        down = p_ref[:, low : low + s.face]
        up = p_ref[:, low + s.own : low + s.own + s.face]
        at = slice(c * s.face, (c + 1) * s.face)
        to_a, to_b = jnp.where(even, up, down), jnp.where(even, down, up)
        for i in range(za_ref.shape[0]):
            za_ref[i, :, at] = to_a[4 * i : 4 * i + 4]
            zb_ref[i, :, at] = to_b[4 * i : 4 * i + 4]


def fold_z_kernel(s, p_ref, ra_ref, rb_ref, o_ref, ya_ref, yb_ref):
    below, above, even = place("gz")
    layer = iota((s.bp, s.per), 1) // s.cx
    first = jnp.where(below, 0, 1)
    last = jnp.where(above, s.cz + 2, s.cz)
    inside = (layer >= first) & (layer <= last)
    shared = iota((4, s.face), 1) < s.used
    for c in range(3):
        low = c * s.per
        high = low + s.own
        at = slice(c * s.face, (c + 1) * s.face)
        o_ref[:, low : low + s.per] = jnp.where(inside, p_ref[:, low : low + s.per], 0.0)
        for i in range(ra_ref.shape[0]):
            rows = slice(4 * i, 4 * i + 4)
            up, down = from_sides(even, ra_ref[i, :, at], rb_ref[i, :, at])
            o_ref[rows, low : low + s.face] += jnp.where(shared & below, down, 0.0)
            o_ref[rows, high : high + s.face] += jnp.where(shared & above, up, 0.0)
    even = place("gy")[2]
    down, up = o_ref[:4, :], o_ref[s.cy : s.cy + 4, :]
    ya_ref[...] = jnp.where(even, up, down)
    yb_ref[...] = jnp.where(even, down, up)


def fold_y(s, p_ref, ra_ref, rb_ref, v_ref):
    below, above, even = place("gy")
    up, down = from_sides(even, ra_ref[...], rb_ref[...])
    row = iota((s.bp, s.wide), 0)
    inside = (row >= jnp.where(below, 0, 1)) & (row <= jnp.where(above, s.cy + 2, s.cy))
    v_ref[...] = jnp.where(inside, p_ref[...], 0.0)
    shared = iota((4, s.wide), 0) < REACH
    v_ref[:4, :] += jnp.where(shared & below, down, 0.0)
    v_ref[s.cy : s.cy + 4, :] += jnp.where(shared & above, up, 0.0)


def own_part(s, v_ref, out_ref):
    for c in range(3):
        rows = v_ref[1 : s.cy + 1, c * s.per : (c + 1) * s.per]
        out_ref[:, c * s.own : (c + 1) * s.own] = roll(rows, -s.cx)[:, : s.own]


def operate(s, v_ref, yd_ref, rd_ref, re_ref, grads, scratch):
    even_ref, odd_ref, *pairs, acc_ref = scratch
    cells = []
    for zc in range(s.cz):
        for c in range(3):
            lanes = v_ref[:, c * s.per : (c + 1) * s.per]
            cell = roll(lanes, -zc * s.cx)[:, : s.tap]
            group = iota(cell.shape, 1) // s.cx % 2
            back = jnp.where(group == 0, roll(cell, s.cx), roll(cell, 3 * s.cx))
            cells += [cell + back, cell - back]
    ph, plow = split(jnp.concatenate(cells, 1))
    inner = dot(yd_ref[...], jnp.concatenate([ph, plow, ph], 0))
    for i in range(3 * s.cz):
        at = slice(i * s.sy, (i + 1) * s.sy)
        for j, ref in enumerate((even_ref, odd_ref)):
            low = (2 * i + j) * s.tap
            ref[at, :] = jnp.concatenate(split(inner[:, low : low + s.tap]), 1)
    gz_inner, gz_edge, gy_ref, gs_ref, gx_ref = grads
    square = jnp.zeros((16, s.nx), F32)
    half = SPACING // 2
    for k in range(half):
        fe_ref, fo_ref, w0, w1 = pairs[4 * (k % 2) : 4 * (k % 2) + 4]
        fe_ref[...] = dot(even_ref[...], rd_ref[k])
        fo_ref[...] = dot(odd_ref[...], rd_ref[half + k])
        for zc in range(s.cz):
            for y in range(0, s.sy, 16):
                rows = slice(y, y + 16)
                at = [
                    slice((zc * 3 + c) * s.sy + y, (zc * 3 + c) * s.sy + y + 16) for c in range(3)
                ]
                even = [fe_ref[i, :] for i in at]
                odd = [fo_ref[i, :] for i in at]
                for sign, v, w_ref in ((1, k, w0), (-1, SPACING - 1 - k, w1)):
                    z = zc * SPACING + v
                    if z < REACH:
                        gz_ref, iz = gz_edge, z
                    elif z >= s.sz - REACH:
                        gz_ref, iz = gz_edge, REACH + z - (s.sz - REACH)
                    else:
                        gz_ref, iz = gz_inner, z - REACH
                    g = [gz_ref[iz, rows], gy_rows(s, gy_ref, gs_ref, z, rows), gx_ref[z, rows]]
                    f = [e + o if sign > 0 else e - o for e, o in zip(even, odd)]
                    dotted = g[0] * f[0] + g[1] * f[1] + g[2] * f[2]
                    square = square + dotted * dotted
                    for c in range(3):
                        w_ref[at[c], :] = (g[c] * dotted).astype(BF16)
        add = dot(
            jnp.concatenate([w0[...], w1[...]], 1),
            jnp.concatenate([re_ref[k], re_ref[SPACING - 1 - k]], 0),
        )
        acc_ref[...] = add if k == 0 else acc_ref[...] + add
    return square


def square_tile(square):
    total = square[:8] + square[8:]
    return sum(total[:, i : i + LANES] for i in range(0, total.shape[1], LANES))


def tile_of(own):
    square = own * own
    return sum(square[:, i : i + LANES] for i in range(0, own.shape[1], LANES))


def total_of(value):
    return jnp.sum(value, keepdims=True)


def moments(sums):
    lane = iota((1, LANES), 1)
    out = jnp.zeros((1, LANES), F32)
    for k, value in enumerate(sums):
        out = jnp.where(lane == k, value, out)
    return out


def apply_kernel(
    s, p_ref, ra_ref, rb_ref, gi_ref, ge_ref, gy_ref, gs_ref, gx_ref, yd_ref, rd_ref, ye_ref, re_ref,
    o_ref, za_ref, zb_ref, own_ref, sum_ref, v_ref, *scratch,
):
    fold_y(s, p_ref, ra_ref, rb_ref, v_ref)
    own_part(s, v_ref, own_ref)
    square = operate(
        s, v_ref, yd_ref, rd_ref, re_ref, (gi_ref, ge_ref, gy_ref, gs_ref, gx_ref), scratch
    )
    encode_y(s, lambda i: scratch[-1][i * s.sy : (i + 1) * s.sy, :], ye_ref, o_ref)
    send_faces(s, o_ref, za_ref, zb_ref)
    sum_ref[0] = tile_of(own_ref[...])
    sum_ref[1] = square_tile(square)


NEIGHBOURS = [(dz, dy) for dz in (-1, 0, 1) for dy in (-1, 0, 1) if dz or dy]


def neighbour(dz, dy):
    nz, ny = lax.axis_size("gz"), lax.axis_size("gy")
    iz, iy = lax.axis_index("gz"), lax.axis_index("gy")
    tz, ty = iz + dz, iy + dy
    ok = (tz >= 0) & (tz < nz) & (ty >= 0) & (ty < ny)
    return ok, jnp.where(ok, tz * ny + ty, iz * ny + iy)


def last_kernel(
    s, p_ref, ra_ref, rb_ref, gi_ref, ge_ref, gy_ref, gs_ref, gx_ref, m_ref,
    yd_ref, rd_ref, ye_ref, re_ref,
    own_ref, part_ref, send_ref, v_ref, o_ref, t_ref, y_ref, *scratch,
):
    fold_y(s, p_ref, ra_ref, rb_ref, v_ref)
    own_part(s, v_ref, own_ref)
    square = operate(
        s, v_ref, yd_ref, rd_ref, re_ref, (gi_ref, ge_ref, gy_ref, gs_ref, gx_ref), scratch
    )
    own = own_ref[...]
    parts = [m_ref[0], m_ref[1], tile_of(own), square_tile(square)]
    sums = moments([total_of(v) for v in parts])
    encode_y(s, lambda i: scratch[-1][i * s.sy : (i + 1) * s.sy, :], ye_ref, o_ref)
    own_part(s, o_ref, part_ref)
    for d in range(send_ref.shape[0]):
        send_ref[d, s.block - 1, :, :] = sums
    lane = iota((s.bp, 2 * LANES), 1)
    t_ref[...] = jnp.zeros_like(t_ref)
    for i, dz in enumerate((-1, 1)):
        layer = 0 if dz < 0 else s.cz + 1
        width = s.cx if dz < 0 else s.pair
        total = jnp.zeros((s.bp, 2 * LANES), F32)
        for c in range(3):
            low = c * s.pair
            lanes = roll(o_ref[:, c * s.per : (c + 1) * s.per], low - layer * s.cx)
            total = jnp.where((lane >= low) & (lane < low + width), lanes[:, : 2 * LANES], total)
        t_ref[i, 8 : 8 + s.bp, :] = total
    for c in range(3):
        lanes = roll(o_ref[:, c * s.per : (c + 1) * s.per], -s.cx)
        y_ref[:, c * s.own : (c + 1) * s.own] = lanes[:, : s.own]
    half = s.cy // 2
    low_half = iota((half, LANES), 1) < LANES // 2
    for dz, dy in NEIGHBOURS:
        _, target = neighbour(dz, dy)
        if dz:
            start = 9 + dy * s.cy
            side = (dz + 1) // 2
            send_ref[target, 0 : s.cy, 0, :] = t_ref[side, start : start + s.cy, :LANES]
            near = t_ref[side, start : start + half, LANES:]
            far = t_ref[side, start + half : start + s.cy, LANES:]
            send_ref[target, s.cy : s.cy + half, 0, :] = jnp.where(
                low_half, near, roll(far, LANES // 2)
            )
        else:
            for c in range(3):
                lanes = slice(c * s.own, (c + 1) * s.own)
                if dy > 0:
                    send_ref[target, 2 * c : 2 * c + 2, 0, :] = y_ref[s.cy + 1 : s.cy + 3, lanes]
                else:
                    send_ref[target, c, :, :] = y_ref[0:1, lanes]


def finish_kernel(s, v0_ref, v1_ref, part_ref, got_ref, u_ref, r_ref, v_ref, t_ref, w_ref):
    v_ref[...] = part_ref[...]
    half = s.cy // 2
    for i, dz in enumerate((-1, 1)):
        first = jnp.zeros((s.cy, LANES), F32)
        rest = jnp.zeros((half, LANES), F32)
        for dy in (-1, 0, 1):
            ok, source = neighbour(dz, dy)
            first += jnp.where(ok, got_ref[source, 0 : s.cy, 0, :], 0.0)
            rest += jnp.where(ok, got_ref[source, s.cy : s.cy + half, 0, :], 0.0)
        t_ref[i] = first
        w_ref[i, 0:half, :] = rest
        w_ref[i, half:, :] = roll(rest, LANES // 2)

    lane = iota((s.cy, s.own), 1)
    for c in range(3):
        lanes = slice(c * s.own, (c + 1) * s.own)
        first, last = (w_ref[0], w_ref[1]) if c == 2 else (t_ref[0], t_ref[1])
        low = c % 2 * s.pair
        v_ref[:, lanes] += jnp.where(lane < s.pair, roll(first, -low), 0.0)
        last = roll(last, (s.cz - 1) * s.cx - low)
        v_ref[:, lanes] += jnp.where(lane >= s.own - s.cx, last, 0.0)
    for dy in (-1, 1):
        ok, source = neighbour(0, dy)
        for c in range(3):
            lanes = slice(c * s.own, (c + 1) * s.own)
            if dy < 0:
                value = got_ref[source, 2 * c : 2 * c + 2, 0, :]
                v_ref[0:2, lanes] += jnp.where(ok, value, 0.0)
            else:
                v_ref[s.cy - 1 : s.cy, lanes] += jnp.where(ok, got_ref[source, c, :, :], 0.0)

    tot = jnp.sum(got_ref[:, s.block - 1, 0, :], axis=0, keepdims=True)
    m0, m1, m2, m3 = (tot[:, k : k + 1] for k in range(4))
    v0, v1, v2 = v0_ref[...], v1_ref[...], v_ref[...]
    rho = m1 / m0
    a0 = 1.0 / (rho + DAMPING)
    rr1 = a0 * a0 * (m2 - rho * m1)
    beta = rr1 / m0
    quad = a0 * a0 * (m3 - 2.0 * rho * m2 + rho * rho * m1) + DAMPING * rr1
    a1 = rr1 / (quad - beta * rr1 / a0)
    r1 = a0 * (rho * v0 - v1)
    image = a0 * (rho * v1 - v2) + DAMPING * r1 + beta * (v1 + DAMPING * v0)
    update = a0 * v0 + a1 * (r1 + beta * v0)
    residual = r1 - a1 * image
    for out_ref, value in ((u_ref, update), (r_ref, residual)):
        for c in range(3):
            for a in range(s.cz):
                at = c * s.own + a * s.cx
                out_ref[c, a] = value[:, at : at + s.cx]


def swap(value_a, value_b, axis):
    count = lax.axis_size(axis)
    even = [(i, i ^ 1) for i in range(count)]
    odd = [(i, (i + (1 if i % 2 else -1)) % count) for i in range(count)]
    value_b = lax.ppermute(value_b, axis, odd)
    return lax.ppermute(value_a, axis, even), value_b


def scratch_of(item):
    if not isinstance(item, tuple):
        return item
    return pltpu.VMEM(*(item if isinstance(item[0], tuple) else (item, F32)))


def call(kernel, outs, scratch, *args, far=0):
    shapes = [jax.ShapeDtypeStruct(o, F32) for o in outs]
    return pl.pallas_call(
        kernel,
        out_shape=shapes,
        in_specs=[HBM] * far + [VMEM] * (len(args) - far),
        out_specs=[VMEM] * len(outs),
        scratch_shapes=[scratch_of(n) for n in scratch],
        compiler_params=PARAMS,
    )(*[pltpu.with_memory_space_constraint(v, pltpu.HBM) for v in args[:far]], *args[far:])


def shards(fixed, moving):
    s = Sizes(fixed.shape)
    devices = lax.axis_size("gz") * lax.axis_size("gy")
    dx, dy, dy_halo = gradient_consts(s)
    yd, rd, ye, re = consts(s)
    part = functools.partial

    zhalo, yhalo = (REACH, s.sy, s.nx), (REACH, s.sz, s.nx)
    za, zb = call(
        part(faces_z_kernel, s),
        [zhalo, zhalo],
        [(2, 2, *zhalo), pltpu.SemaphoreType.DMA((2, 2))],
        fixed, moving, far=2,
    )
    za, zb = swap(za, zb, "gz")
    ya, yb = call(part(faces_y_kernel, s), [yhalo, yhalo], [], fixed, moving)
    ya, yb = swap(ya, yb, "gy")
    volume = fixed.shape
    total, diff, gx, gz_inner = call(
        part(start_kernel, s),
        [volume, volume, volume, (s.sz - 2 * REACH, s.sy, s.nx)],
        [],
        fixed, moving, dx,
    )
    acc = (s.cells, 2 * s.tap)
    half = ((s.cells, s.nx), BF16)

    def rows_of(count):
        rows = 3 * s.cz * count
        return (rows, 2 * s.tap), [((rows, s.nx), BF16)] * 4

    sides = (s.sz, 16, s.nx)
    mid_acc, mid_work = rows_of(s.sy - 32)
    gy, raw, inner = call(
        part(inner_kernel, s), [volume, sides, mid_acc], mid_work,
        total, diff, gx, gz_inner, dy, re,
    )
    side_acc, side_work = rows_of(32)
    gy_side, side = call(
        part(side_kernel, s), [sides, side_acc], [sides, *side_work],
        diff, gx, gz_inner, gy, raw, ya, yb, dy_halo, re,
    )
    grid, zface, yface = (s.bp, s.wide), (round_up(s.nb, 4) // 4, 4, 3 * s.face), (4, s.wide)
    few = ((2 * REACH * 3 * s.sy, s.nx), BF16)
    gz_edge, grid0, za, zb = call(
        part(edge_kernel, s),
        [(2 * REACH, s.sy, s.nx), grid, zface, zface],
        [(2 * REACH, s.sy, s.nx), few, few, (2 * 3 * s.sy, 2 * s.tap)],
        total, diff, gx, gy, gy_side, za, zb, inner, side, ye, re,
    )

    def fold_z(value, za, zb):
        za, zb = swap(za, zb, "gz")
        value, ya, yb = call(part(fold_z_kernel, s), [grid, yface, yface], [], value, za, zb)
        return (value, *swap(ya, yb, "gy"))

    own = (s.cy, 3 * s.own)
    field = (s.cells, s.nx)
    left = ((s.cells, 2 * s.tap), BF16)
    work = [left, left, *[field, field, half, half] * 2, acc]
    grads = (gz_inner, gz_edge, gy, gy_side, gx)
    grid1, za, zb, v0, sums = call(
        part(apply_kernel, s),
        [grid, zface, zface, own, (2, s.cy, LANES)],
        [grid, *work],
        *fold_z(grid0, za, zb), *grads, yd, rd, ye, re,
    )
    v1, mine, send = call(
        part(last_kernel, s),
        [own, own, (devices, s.block, 1, LANES)],
        [grid, grid, (2, 16 + s.bp, 2 * LANES), (s.bp, 3 * s.own), *work],
        *fold_z(grid1, za, zb), *grads, sums, yd, rd, ye, re,
    )
    got = lax.all_to_all(send, ("gz", "gy"), 0, 0)
    out = (3, s.cz, s.cy, s.cx)
    return tuple(
        call(
            part(finish_kernel, s), [out, out], [own, (2, s.cy, LANES), (2, s.cy, LANES)], v0, v1, mine, got
        )
    )


def solution(mesh):
    return jax.shard_map(
        shards,
        mesh=mesh,
        in_specs=(P("gz", "gy", None), P("gz", "gy", None)),
        out_specs=(P(None, "gz", "gy", None), P(None, "gz", "gy", None)),
        check_vma=False,
    )
```

```python
import functools

import jax
import jax.numpy as jnp
import numpy as np
from jax import lax
from jax.experimental import pallas as pl
from jax.experimental.pallas import tpu as pltpu
from jax.sharding import PartitionSpec as P


SPACING = 8
DAMPING = 8.0
LANES = 128
REACH = 3
F32 = jnp.float32
BF16 = jnp.bfloat16
VMEM = pl.BlockSpec(memory_space=pltpu.VMEM)
HBM = pl.BlockSpec(memory_space=pltpu.MemorySpace.HBM)
VMEM_LIMIT = 20 * 1024 * 1024
PARAMS = pltpu.CompilerParams(vmem_limit_bytes=VMEM_LIMIT)
SPREAD = pltpu.CompilerParams(vmem_limit_bytes=VMEM_LIMIT)


def round_up(value, step):
    return -(-value // step) * step


class Sizes:
    def __init__(self, shape):
        self.sz, self.sy, self.nx = shape
        self.cz, self.cy, self.cx = (n // SPACING for n in shape)
        self.na, self.nb = self.cz + 3, self.cy + 3
        self.bp = round_up(self.nb, 16)
        self.per = round_up(self.na * self.cx, LANES)
        self.wide = 3 * self.per
        self.tap = 4 * self.cx
        self.face = round_up(REACH * self.cx, LANES)
        self.used = REACH * self.cx
        self.own = self.cz * self.cx
        self.cells = 3 * self.cz * self.sy
        self.pair = 2 * self.cx
        assert 2 * 3 * self.pair == 3 * LANES and self.own == LANES
        self.block = self.cy + self.cy // 2 + 1
        assert self.tap % LANES == 0 and self.own % LANES == 0
        assert self.cy % 8 == 0 and self.bp == self.cy + 8 and self.cz > 1
        assert self.sy % 16 == 0 and self.sy > 32


def taps():
    t = (np.arange(SPACING) + 0.5) / SPACING
    return np.stack(
        [
            (1 - t) ** 3 / 6,
            (3 * t**3 - 6 * t**2 + 4) / 6,
            (-3 * t**3 + 3 * t**2 + 3 * t + 1) / 6,
            t**3 / 6,
        ]
    )


def basis(count, columns, offset):
    w = taps()
    out = np.zeros((count, columns))
    for v in range(count):
        for k in range(4):
            col = v // SPACING - 1 + k + offset
            if 0 <= col < columns:
                out[v, col] += w[k, v % SPACING]
    return out


def halves(matrix):
    high = np.asarray(matrix, np.float32).astype(jnp.bfloat16)
    low = (matrix - high.astype(np.float64)).astype(np.float32).astype(jnp.bfloat16)
    return high, low


def consts(s):
    by = basis(s.sy, s.bp, 1)
    yh, yl = halves(by)
    y_decode = np.concatenate([yh, yh, yl], 1)
    y_encode = np.concatenate([yh.T, yh.T, yl.T], 1)
    bx = basis(s.nx, s.cx, 0)
    w = taps()
    decode, encode = [], []
    for k in range(SPACING):
        high, low = halves(np.concatenate([w[t, k] * bx.T for t in range(4)], 0))
        encode.append(np.concatenate([high.T, low.T], 1))
    for sign in (1.0, -1.0):
        for k in range(SPACING // 2):
            parts = [0.5 * (w[t, k] + sign * w[3 - t, k]) * bx.T for t in range(2)]
            (h0, l0), (h1, l1) = (halves(v) for v in parts)
            flip = np.asarray(sign, jnp.bfloat16)
            zero = np.zeros((2 * s.cx, s.nx), jnp.bfloat16)
            decode.append(np.concatenate([h0, h1, flip * l1, flip * l0, h0, h1, zero], 0))
    return tuple(jnp.asarray(v) for v in (y_decode, np.stack(decode), y_encode, np.stack(encode)))


def gradient_consts(s):
    coef = {-3: -1.0, -2: 9.0, -1: -45.0, 1: 45.0, 2: -9.0, 3: 1.0}
    dx = np.zeros((s.nx, s.nx))
    for x in range(s.nx):
        for d, value in coef.items():
            if 0 <= x + d < s.nx:
                dx[x + d, x] = value
    dy = np.zeros((s.sy, s.sy + 16))
    for y in range(s.sy):
        for d, value in coef.items():
            at = y + d
            if at < 0:
                dy[y, s.sy + REACH + at] = value
            elif at >= s.sy:
                dy[y, s.sy + REACH + at - s.sy] = value
            else:
                dy[y, at] = value
    own, halo = dy[:, : s.sy], dy[:, s.sy :]
    halo = np.concatenate([halo[:8], halo[-8:]], 0)
    pairs = (np.concatenate([dx, dx], 0), *(np.concatenate([v, v], 1) for v in (own, halo)))
    return tuple(jnp.asarray(v.astype(jnp.bfloat16)) for v in pairs)


def split(value):
    high = value.astype(BF16)
    return high, (value - high.astype(F32)).astype(BF16)


def dot(a, b):
    return jnp.dot(a, b, preferred_element_type=F32)


def rounded(value):
    return (value * F32(1.0 / 120.0)).astype(BF16).astype(F32)


def place(axis):
    index = lax.axis_index(axis)
    count = lax.axis_size(axis)
    return index > 0, index < count - 1, lax.rem(index, 2) == 0


def from_sides(even, a, b):
    return jnp.where(even, a, b), jnp.where(even, b, a)


def difference(near):
    return (
        45.0 * (near(1) - near(-1)) - 9.0 * (near(2) - near(-2)) + (near(3) - near(-3))
    )


def iota(shape, dim):
    return lax.broadcasted_iota(jnp.int32, shape, dim)


def roll(value, shift):
    shift = shift % value.shape[1]
    return pltpu.roll(value, shift, 1) if shift else value


def start_all(copies):
    for copy in copies:
        copy.start()
    return copies


def faces_z_kernel(s, f_ref, m_ref, za_ref, zb_ref, t_ref, sems):
    copies = []
    for i, ref in enumerate((f_ref, m_ref)):
        for j in range(2):
            z = pl.ds(j * (s.sz - REACH), REACH)
            copies.append(pltpu.make_async_copy(ref.at[z], t_ref.at[i, j], sems.at[i, j]))
    for copy in start_all(copies):
        copy.wait()
    even = place("gz")[2]
    down, up = (t_ref[0, j] + t_ref[1, j] for j in range(2))
    za_ref[...] = jnp.where(even, up, down)
    zb_ref[...] = jnp.where(even, down, up)


def faces_y_kernel(s, f_ref, m_ref, ya_ref, yb_ref):
    even = place("gy")[2]
    for k in range(REACH):
        high = s.sy - REACH + k
        down = f_ref[:, k, :] + m_ref[:, k, :]
        up = f_ref[:, high, :] + m_ref[:, high, :]
        ya_ref[k] = jnp.where(even, up, down)
        yb_ref[k] = jnp.where(even, down, up)


GROUP = 4


def start_kernel(s, f_ref, m_ref, dx_ref, sum_ref, diff_ref, gx_ref, gz_ref):
    dx = dx_ref[...]
    for i in range(s.sz // GROUP):
        planes = slice(i * GROUP, (i + 1) * GROUP)
        f, m = f_ref[planes], m_ref[planes]
        total = f + m
        sum_ref[planes] = total
        diff_ref[planes] = f - m
        sh, sl = split(total.reshape(GROUP * s.sy, s.nx))
        gx = rounded(dot(jnp.concatenate([sh, sl], 1), dx))
        gx_ref[planes] = gx.reshape(GROUP, s.sy, s.nx)

    def step(i, carry):
        for y in range(0, s.sy, 16):
            rows = slice(y, y + 16)
            gz_ref[i, rows] = rounded(difference(lambda d: sum_ref[i + REACH + d, rows]))
        return carry

    lax.fori_loop(0, s.sz - 2 * REACH, step, 0)


def edge_planes(s):
    return [z < REACH or z >= s.sz - REACH for z in range(s.sz)]


def put_volume(row_of, z, rows, diff_ref, grads, high_ref, low_ref):
    mm = diff_ref[z, rows]
    for c in range(3):
        high, low = split(mm * grads[c])
        at = slice(row_of(c), row_of(c) + rows.stop - rows.start)
        high_ref[at, :] = high
        low_ref[at, :] = low


def gy_rows(s, gy_ref, side_ref, z, rows):
    if rows.start == 0:
        return jnp.concatenate([side_ref[z, :8], gy_ref[z, 8:16]], 0)
    if rows.stop == s.sy:
        return jnp.concatenate([gy_ref[z, s.sy - 16 : s.sy - 8], side_ref[z, 8:]], 0)
    return gy_ref[z, rows]


def encode_planes(s, starts, diff_ref, gx_ref, gz_ref, gy_of, re_ref, acc_ref, scratch):
    waits = edge_planes(s)
    count = 16 * len(starts)
    part = 3 * count
    acc_ref[...] = jnp.zeros_like(acc_ref)
    for k in range(SPACING):
        vh, vl = scratch[2 * (k % 2) : 2 * (k % 2) + 2]
        ready = [zc for zc in range(s.cz) if not waits[zc * SPACING + k]]
        for zc in ready:
            z = zc * SPACING + k
            for i, y in enumerate(starts):
                rows = slice(y, y + 16)
                grads = [gz_ref[z - REACH, rows], gy_of(z, rows), gx_ref[z, rows]]
                base = zc * part + 16 * i
                put_volume(lambda c: base + c * count, z, rows, diff_ref, grads, vh, vl)
        at = slice(ready[0] * part, (ready[-1] + 1) * part)
        weights = re_ref[k]
        acc_ref[at, :] += dot(
            jnp.concatenate([vh[at, :], vl[at, :]], 1), jnp.concatenate([weights, weights], 0)
        )


def inner_kernel(
    s, sum_ref, diff_ref, gx_ref, gz_ref, dy_ref, re_ref, gy_ref, raw_ref, acc_ref, *scratch
):
    dy = dy_ref[...]

    def step(i, carry):
        for j in range(GROUP):
            z = i * GROUP + j
            sh, sl = split(sum_ref[z])
            value = dot(dy, jnp.concatenate([sh, sl], 0))
            raw_ref[z] = jnp.concatenate([value[:8], value[s.sy - 8 :]], 0)
            gy_ref[z] = rounded(value)
        return carry

    lax.fori_loop(0, s.sz // GROUP, step, 0)
    starts = range(16, s.sy - 16, 16)
    encode_planes(
        s, starts, diff_ref, gx_ref, gz_ref, lambda z, rows: gy_ref[z, rows], re_ref, acc_ref, scratch
    )


def side_kernel(
    s, diff_ref, gx_ref, gz_ref, gy_ref, raw_ref, ra_ref, rb_ref, dy_ref, re_ref,
    side_ref, acc_ref, h_ref, *scratch,
):
    below, above, even = place("gy")
    h_ref[...] = jnp.zeros_like(h_ref)
    for k in range(REACH):
        up, down = from_sides(even, ra_ref[k], rb_ref[k])
        h_ref[:, k, :] = jnp.where(below, down, 0.0)
        h_ref[:, REACH + k, :] = jnp.where(above, up, 0.0)
    dy = dy_ref[...]

    def step(i, carry):
        for j in range(GROUP):
            z = i * GROUP + j
            add = dot(dy, jnp.concatenate(split(h_ref[z]), 0))
            side_ref[z] = rounded(raw_ref[z] + add)
        return carry

    lax.fori_loop(0, s.sz // GROUP, step, 0)
    encode_planes(
        s, (0, s.sy - 16), diff_ref, gx_ref, gz_ref,
        lambda z, rows: gy_rows(s, gy_ref, side_ref, z, rows), re_ref, acc_ref, scratch,
    )


def edge_kernel(
    s, sum_ref, diff_ref, gx_ref, gy_ref, gs_ref, ra_ref, rb_ref, mid_ref, side_ref, ye_ref, re_ref,
    gz_ref, p_ref, za_ref, zb_ref, h_ref, vh_ref, vl_ref, acc_ref,
):
    below, above, even = place("gz")
    for k in range(REACH):
        up, down = from_sides(even, ra_ref[k], rb_ref[k])
        h_ref[k] = jnp.where(below, down, 0.0)
        h_ref[REACH + k] = jnp.where(above, up, 0.0)
    part = 3 * s.sy
    for side in (0, 1):
        first = 0 if side == 0 else s.sz - REACH
        for j in range(REACH):
            z = first + j
            for y in range(0, s.sy, 16):
                rows = slice(y, y + 16)

                def near(d):
                    if z + d < 0:
                        return h_ref[z + d + REACH, rows]
                    if z + d >= s.sz:
                        return h_ref[REACH + z + d - s.sz, rows]
                    return sum_ref[z + d, rows]

                gz = rounded(difference(near))
                gz_ref[side * REACH + j, rows] = gz
                row = (side * REACH + j) * part + y
                grads = [gz, gy_rows(s, gy_ref, gs_ref, z, rows), gx_ref[z, rows]]
                put_volume(lambda c: row + c * s.sy, z, rows, diff_ref, grads, vh_ref, vl_ref)
        lhs, rhs = [], []
        for j in range(REACH):
            row = (side * REACH + j) * part
            weights = re_ref[(first + j) % SPACING]
            for ref in (vh_ref, vl_ref):
                lhs.append(ref[row : row + part, :])
                rhs.append(weights)
        at = slice(side * part, (side + 1) * part)
        acc_ref[at, :] = dot(jnp.concatenate(lhs, 1), jnp.concatenate(rhs, 0))

    def rows_of(i):
        inner = s.sy - 32
        both = jnp.concatenate(
            [
                side_ref[32 * i : 32 * i + 16, :],
                mid_ref[inner * i : inner * (i + 1), :],
                side_ref[32 * i + 16 : 32 * i + 32, :],
            ],
            0,
        )
        zc, c = divmod(i, 3)
        if zc in (0, s.cz - 1):
            row = (3 * (zc > 0) + c) * s.sy
            both = both + acc_ref[row : row + s.sy, :]
        return both

    encode_y(s, rows_of, ye_ref, p_ref)
    send_faces(s, p_ref, za_ref, zb_ref)


def encode_y(s, rows_of, ye_ref, p_ref):
    columns = []
    for i in range(3 * s.cz):
        both = rows_of(i)
        columns.append(both[:, : s.tap] + both[:, s.tap :])
    high, low = split(jnp.concatenate(columns, 1))
    out = dot(ye_ref[...], jnp.concatenate([high, low, high], 0))
    for c in range(3):
        total = jnp.zeros((s.bp, s.per), F32)
        for zc in range(s.cz):
            at = (zc * 3 + c) * s.tap
            cell = out[:, at : at + s.tap]
            if s.per > s.tap:
                cell = jnp.concatenate([cell, jnp.zeros((s.bp, s.per - s.tap), F32)], 1)
            total = total + roll(cell, zc * s.cx)
        p_ref[:, c * s.per : (c + 1) * s.per] = total


def send_faces(s, p_ref, za_ref, zb_ref):
    even = place("gz")[2]
    for c in range(3):
        low = c * s.per
        down = p_ref[:, low : low + s.face]
        up = p_ref[:, low + s.own : low + s.own + s.face]
        at = slice(c * s.face, (c + 1) * s.face)
        to_a, to_b = jnp.where(even, up, down), jnp.where(even, down, up)
        for i in range(za_ref.shape[0]):
            za_ref[i, :, at] = to_a[4 * i : 4 * i + 4]
            zb_ref[i, :, at] = to_b[4 * i : 4 * i + 4]


def fold_z_kernel(s, p_ref, ra_ref, rb_ref, o_ref, ya_ref, yb_ref):
    below, above, even = place("gz")
    layer = iota((s.bp, s.per), 1) // s.cx
    first = jnp.where(below, 0, 1)
    last = jnp.where(above, s.cz + 2, s.cz)
    inside = (layer >= first) & (layer <= last)
    shared = iota((4, s.face), 1) < s.used
    for c in range(3):
        low = c * s.per
        high = low + s.own
        at = slice(c * s.face, (c + 1) * s.face)
        o_ref[:, low : low + s.per] = jnp.where(inside, p_ref[:, low : low + s.per], 0.0)
        for i in range(ra_ref.shape[0]):
            rows = slice(4 * i, 4 * i + 4)
            up, down = from_sides(even, ra_ref[i, :, at], rb_ref[i, :, at])
            o_ref[rows, low : low + s.face] += jnp.where(shared & below, down, 0.0)
            o_ref[rows, high : high + s.face] += jnp.where(shared & above, up, 0.0)
    even = place("gy")[2]
    down, up = o_ref[:4, :], o_ref[s.cy : s.cy + 4, :]
    ya_ref[...] = jnp.where(even, up, down)
    yb_ref[...] = jnp.where(even, down, up)


def fold_y(s, p_ref, ra_ref, rb_ref, v_ref):
    below, above, even = place("gy")
    up, down = from_sides(even, ra_ref[...], rb_ref[...])
    row = iota((s.bp, s.wide), 0)
    inside = (row >= jnp.where(below, 0, 1)) & (row <= jnp.where(above, s.cy + 2, s.cy))
    v_ref[...] = jnp.where(inside, p_ref[...], 0.0)
    shared = iota((4, s.wide), 0) < REACH
    v_ref[:4, :] += jnp.where(shared & below, down, 0.0)
    v_ref[s.cy : s.cy + 4, :] += jnp.where(shared & above, up, 0.0)


def own_part(s, v_ref, out_ref):
    for c in range(3):
        rows = v_ref[1 : s.cy + 1, c * s.per : (c + 1) * s.per]
        out_ref[:, c * s.own : (c + 1) * s.own] = roll(rows, -s.cx)[:, : s.own]


def operate(s, v_ref, yd_ref, rd_ref, re_ref, grads, scratch):
    even_ref, odd_ref, *pairs, acc_ref = scratch
    cells = []
    for zc in range(s.cz):
        for c in range(3):
            lanes = v_ref[:, c * s.per : (c + 1) * s.per]
            cell = roll(lanes, -zc * s.cx)[:, : s.tap]
            group = iota(cell.shape, 1) // s.cx % 2
            back = jnp.where(group == 0, roll(cell, s.cx), roll(cell, 3 * s.cx))
            cells += [cell + back, cell - back]
    ph, plow = split(jnp.concatenate(cells, 1))
    inner = dot(yd_ref[...], jnp.concatenate([ph, plow, ph], 0))
    for i in range(3 * s.cz):
        at = slice(i * s.sy, (i + 1) * s.sy)
        for j, ref in enumerate((even_ref, odd_ref)):
            low = (2 * i + j) * s.tap
            ref[at, :] = jnp.concatenate(split(inner[:, low : low + s.tap]), 1)
    gz_inner, gz_edge, gy_ref, gs_ref, gx_ref = grads
    square = jnp.zeros((16, s.nx), F32)
    half = SPACING // 2
    for k in range(half):
        fe_ref, fo_ref, w0, w1 = pairs[4 * (k % 2) : 4 * (k % 2) + 4]
        fe_ref[...] = dot(even_ref[...], rd_ref[k])
        fo_ref[...] = dot(odd_ref[...], rd_ref[half + k])
        for zc in range(s.cz):
            for y in range(0, s.sy, 16):
                rows = slice(y, y + 16)
                at = [
                    slice((zc * 3 + c) * s.sy + y, (zc * 3 + c) * s.sy + y + 16) for c in range(3)
                ]
                even = [fe_ref[i, :] for i in at]
                odd = [fo_ref[i, :] for i in at]
                for sign, v, w_ref in ((1, k, w0), (-1, SPACING - 1 - k, w1)):
                    z = zc * SPACING + v
                    if z < REACH:
                        gz_ref, iz = gz_edge, z
                    elif z >= s.sz - REACH:
                        gz_ref, iz = gz_edge, REACH + z - (s.sz - REACH)
                    else:
                        gz_ref, iz = gz_inner, z - REACH
                    g = [gz_ref[iz, rows], gy_rows(s, gy_ref, gs_ref, z, rows), gx_ref[z, rows]]
                    f = [e + o if sign > 0 else e - o for e, o in zip(even, odd)]
                    dotted = g[0] * f[0] + g[1] * f[1] + g[2] * f[2]
                    square = square + dotted * dotted
                    for c in range(3):
                        w_ref[at[c], :] = (g[c] * dotted).astype(BF16)
        add = dot(
            jnp.concatenate([w0[...], w1[...]], 1),
            jnp.concatenate([re_ref[k], re_ref[SPACING - 1 - k]], 0),
        )
        acc_ref[...] = add if k == 0 else acc_ref[...] + add
    return square


def square_tile(square):
    total = square[:8] + square[8:]
    return sum(total[:, i : i + LANES] for i in range(0, total.shape[1], LANES))


def tile_of(own):
    square = own * own
    return sum(square[:, i : i + LANES] for i in range(0, own.shape[1], LANES))


def total_of(value):
    return jnp.sum(value, keepdims=True)


def moments(sums):
    lane = iota((1, LANES), 1)
    out = jnp.zeros((1, LANES), F32)
    for k, value in enumerate(sums):
        out = jnp.where(lane == k, value, out)
    return out


def apply_kernel(
    s, p_ref, ra_ref, rb_ref, gi_ref, ge_ref, gy_ref, gs_ref, gx_ref, yd_ref, rd_ref, ye_ref, re_ref,
    o_ref, za_ref, zb_ref, own_ref, sum_ref, v_ref, *scratch,
):
    fold_y(s, p_ref, ra_ref, rb_ref, v_ref)
    own_part(s, v_ref, own_ref)
    square = operate(
        s, v_ref, yd_ref, rd_ref, re_ref, (gi_ref, ge_ref, gy_ref, gs_ref, gx_ref), scratch
    )
    encode_y(s, lambda i: scratch[-1][i * s.sy : (i + 1) * s.sy, :], ye_ref, o_ref)
    send_faces(s, o_ref, za_ref, zb_ref)
    sum_ref[0] = tile_of(own_ref[...])
    sum_ref[1] = square_tile(square)


NEIGHBOURS = [(dz, dy) for dz in (-1, 0, 1) for dy in (-1, 0, 1) if dz or dy]


def neighbour(dz, dy):
    nz, ny = lax.axis_size("gz"), lax.axis_size("gy")
    iz, iy = lax.axis_index("gz"), lax.axis_index("gy")
    tz, ty = iz + dz, iy + dy
    ok = (tz >= 0) & (tz < nz) & (ty >= 0) & (ty < ny)
    return ok, jnp.where(ok, tz * ny + ty, iz * ny + iy)


def last_kernel(
    s, p_ref, ra_ref, rb_ref, gi_ref, ge_ref, gy_ref, gs_ref, gx_ref, m_ref,
    yd_ref, rd_ref, ye_ref, re_ref,
    own_ref, part_ref, send_ref, v_ref, o_ref, t_ref, y_ref, *scratch,
):
    fold_y(s, p_ref, ra_ref, rb_ref, v_ref)
    own_part(s, v_ref, own_ref)
    square = operate(
        s, v_ref, yd_ref, rd_ref, re_ref, (gi_ref, ge_ref, gy_ref, gs_ref, gx_ref), scratch
    )
    own = own_ref[...]
    parts = [m_ref[0], m_ref[1], tile_of(own), square_tile(square)]
    sums = moments([total_of(v) for v in parts])
    encode_y(s, lambda i: scratch[-1][i * s.sy : (i + 1) * s.sy, :], ye_ref, o_ref)
    own_part(s, o_ref, part_ref)
    for d in range(send_ref.shape[0]):
        send_ref[d, s.block - 1, :, :] = sums
    lane = iota((s.bp, 2 * LANES), 1)
    t_ref[...] = jnp.zeros_like(t_ref)
    for i, dz in enumerate((-1, 1)):
        layer = 0 if dz < 0 else s.cz + 1
        width = s.cx if dz < 0 else s.pair
        total = jnp.zeros((s.bp, 2 * LANES), F32)
        for c in range(3):
            low = c * s.pair
            lanes = roll(o_ref[:, c * s.per : (c + 1) * s.per], low - layer * s.cx)
            total = jnp.where((lane >= low) & (lane < low + width), lanes[:, : 2 * LANES], total)
        t_ref[i, 8 : 8 + s.bp, :] = total
    for c in range(3):
        lanes = roll(o_ref[:, c * s.per : (c + 1) * s.per], -s.cx)
        y_ref[:, c * s.own : (c + 1) * s.own] = lanes[:, : s.own]
    half = s.cy // 2
    low_half = iota((half, LANES), 1) < LANES // 2
    for dz, dy in NEIGHBOURS:
        _, target = neighbour(dz, dy)
        if dz:
            start = 9 + dy * s.cy
            side = (dz + 1) // 2
            send_ref[target, 0 : s.cy, 0, :] = t_ref[side, start : start + s.cy, :LANES]
            near = t_ref[side, start : start + half, LANES:]
            far = t_ref[side, start + half : start + s.cy, LANES:]
            send_ref[target, s.cy : s.cy + half, 0, :] = jnp.where(
                low_half, near, roll(far, LANES // 2)
            )
        else:
            for c in range(3):
                lanes = slice(c * s.own, (c + 1) * s.own)
                if dy > 0:
                    send_ref[target, 2 * c : 2 * c + 2, 0, :] = y_ref[s.cy + 1 : s.cy + 3, lanes]
                else:
                    send_ref[target, c, :, :] = y_ref[0:1, lanes]


def finish_kernel(s, v0_ref, v1_ref, part_ref, got_ref, u_ref, r_ref, v_ref, t_ref, w_ref):
    v_ref[...] = part_ref[...]
    half = s.cy // 2
    for i, dz in enumerate((-1, 1)):
        first = jnp.zeros((s.cy, LANES), F32)
        rest = jnp.zeros((half, LANES), F32)
        for dy in (-1, 0, 1):
            ok, source = neighbour(dz, dy)
            first += jnp.where(ok, got_ref[source, 0 : s.cy, 0, :], 0.0)
            rest += jnp.where(ok, got_ref[source, s.cy : s.cy + half, 0, :], 0.0)
        t_ref[i] = first
        w_ref[i, 0:half, :] = rest
        w_ref[i, half:, :] = roll(rest, LANES // 2)

    lane = iota((s.cy, s.own), 1)
    for c in range(3):
        lanes = slice(c * s.own, (c + 1) * s.own)
        first, last = (w_ref[0], w_ref[1]) if c == 2 else (t_ref[0], t_ref[1])
        low = c % 2 * s.pair
        v_ref[:, lanes] += jnp.where(lane < s.pair, roll(first, -low), 0.0)
        last = roll(last, (s.cz - 1) * s.cx - low)
        v_ref[:, lanes] += jnp.where(lane >= s.own - s.cx, last, 0.0)
    for dy in (-1, 1):
        ok, source = neighbour(0, dy)
        for c in range(3):
            lanes = slice(c * s.own, (c + 1) * s.own)
            if dy < 0:
                value = got_ref[source, 2 * c : 2 * c + 2, 0, :]
                v_ref[0:2, lanes] += jnp.where(ok, value, 0.0)
            else:
                v_ref[s.cy - 1 : s.cy, lanes] += jnp.where(ok, got_ref[source, c, :, :], 0.0)

    tot = jnp.sum(got_ref[:, s.block - 1, 0, :], axis=0, keepdims=True)
    m0, m1, m2, m3 = (tot[:, k : k + 1] for k in range(4))
    v0, v1, v2 = v0_ref[...], v1_ref[...], v_ref[...]
    rho = m1 / m0
    a0 = 1.0 / (rho + DAMPING)
    rr1 = a0 * a0 * (m2 - rho * m1)
    beta = rr1 / m0
    quad = a0 * a0 * (m3 - 2.0 * rho * m2 + rho * rho * m1) + DAMPING * rr1
    a1 = rr1 / (quad - beta * rr1 / a0)
    r1 = a0 * (rho * v0 - v1)
    image = a0 * (rho * v1 - v2) + DAMPING * r1 + beta * (v1 + DAMPING * v0)
    update = a0 * v0 + a1 * (r1 + beta * v0)
    residual = r1 - a1 * image
    for out_ref, value in ((u_ref, update), (r_ref, residual)):
        for c in range(3):
            for a in range(s.cz):
                at = c * s.own + a * s.cx
                out_ref[c, a] = value[:, at : at + s.cx]


def swap(value_a, value_b, axis):
    count = lax.axis_size(axis)
    even = [(i, i ^ 1) for i in range(count)]
    odd = [(i, (i + (1 if i % 2 else -1)) % count) for i in range(count)]
    value_b = lax.ppermute(value_b, axis, odd)
    return lax.ppermute(value_a, axis, even), value_b


def scratch_of(item):
    if not isinstance(item, tuple):
        return item
    return pltpu.VMEM(*(item if isinstance(item[0], tuple) else (item, F32)))


def call(kernel, name, outs, scratch, *args, far=0):
    shapes = [jax.ShapeDtypeStruct(o, F32) for o in outs]
    return pl.pallas_call(
        kernel,
        out_shape=shapes,
        in_specs=[HBM] * far + [VMEM] * (len(args) - far),
        out_specs=[VMEM] * len(outs),
        scratch_shapes=[scratch_of(n) for n in scratch],
        compiler_params=SPREAD if name in ("apply", "last") else PARAMS,
    )(*[pltpu.with_memory_space_constraint(v, pltpu.HBM) for v in args[:far]], *args[far:])


def shards(fixed, moving):
    s = Sizes(fixed.shape)
    devices = lax.axis_size("gz") * lax.axis_size("gy")
    dx, dy, dy_halo = gradient_consts(s)
    yd, rd, ye, re = consts(s)
    part = functools.partial

    zhalo, yhalo = (REACH, s.sy, s.nx), (REACH, s.sz, s.nx)
    za, zb = call(
        part(faces_z_kernel, s),
        "faces_z",
        [zhalo, zhalo],
        [(2, 2, *zhalo), pltpu.SemaphoreType.DMA((2, 2))],
        fixed, moving, far=2,
    )
    za, zb = swap(za, zb, "gz")
    ya, yb = call(part(faces_y_kernel, s), "faces_y", [yhalo, yhalo], [], fixed, moving)
    ya, yb = swap(ya, yb, "gy")
    volume = fixed.shape
    total, diff, gx, gz_inner = call(
        part(start_kernel, s),
        "start",
        [volume, volume, volume, (s.sz - 2 * REACH, s.sy, s.nx)],
        [],
        fixed, moving, dx,
    )
    acc = (s.cells, 2 * s.tap)
    half = ((s.cells, s.nx), BF16)

    def rows_of(count):
        rows = 3 * s.cz * count
        return (rows, 2 * s.tap), [((rows, s.nx), BF16)] * 4

    sides = (s.sz, 16, s.nx)
    mid_acc, mid_work = rows_of(s.sy - 32)
    gy, raw, inner = call(
        part(inner_kernel, s), "inner", [volume, sides, mid_acc], mid_work,
        total, diff, gx, gz_inner, dy, re,
    )
    side_acc, side_work = rows_of(32)
    gy_side, side = call(
        part(side_kernel, s), "side", [sides, side_acc], [sides, *side_work],
        diff, gx, gz_inner, gy, raw, ya, yb, dy_halo, re,
    )
    grid, zface, yface = (s.bp, s.wide), (round_up(s.nb, 4) // 4, 4, 3 * s.face), (4, s.wide)
    few = ((2 * REACH * 3 * s.sy, s.nx), BF16)
    gz_edge, grid0, za, zb = call(
        part(edge_kernel, s),
        "edge",
        [(2 * REACH, s.sy, s.nx), grid, zface, zface],
        [(2 * REACH, s.sy, s.nx), few, few, (2 * 3 * s.sy, 2 * s.tap)],
        total, diff, gx, gy, gy_side, za, zb, inner, side, ye, re,
    )

    def fold_z(value, za, zb):
        za, zb = swap(za, zb, "gz")
        value, ya, yb = call(
            part(fold_z_kernel, s), "fold_z", [grid, yface, yface], [], value, za, zb
        )
        return (value, *swap(ya, yb, "gy"))

    own = (s.cy, 3 * s.own)
    field = (s.cells, s.nx)
    left = ((s.cells, 2 * s.tap), BF16)
    work = [left, left, *[field, field, half, half] * 2, acc]
    grads = (gz_inner, gz_edge, gy, gy_side, gx)
    grid1, za, zb, v0, sums = call(
        part(apply_kernel, s),
        "apply",
        [grid, zface, zface, own, (2, s.cy, LANES)],
        [grid, *work],
        *fold_z(grid0, za, zb), *grads, yd, rd, ye, re,
    )
    v1, mine, send = call(
        part(last_kernel, s),
        "last",
        [own, own, (devices, s.block, 1, LANES)],
        [grid, grid, (2, 16 + s.bp, 2 * LANES), (s.bp, 3 * s.own), *work],
        *fold_z(grid1, za, zb), *grads, sums, yd, rd, ye, re,
    )
    got = lax.all_to_all(send, ("gz", "gy"), 0, 0)
    out = (3, s.cz, s.cy, s.cx)
    return tuple(
        call(
            part(finish_kernel, s), "finish", [out, out], [own, (2, s.cy, LANES), (2, s.cy, LANES)], v0, v1, mine, got
        )
    )


def solution(mesh):
    return jax.shard_map(
        shards,
        mesh=mesh,
        in_specs=(P("gz", "gy", None), P("gz", "gy", None)),
        out_specs=(P(None, "gz", "gy", None), P(None, "gz", "gy", None)),
        check_vma=False,
    )
```
